32 devices in a mesh: groups: 2 (over y), frames: 4 (over z), heads: 2 (over x), pipe: 2 (over core).
Axes of the slice: x: 2, y: 2, z: 4, core: 2. Of those that a mesh axis runs over, the one named last changes fastest.
Arguments:
- query: bfloat16 [4, 1536, 3072], P(('groups', 'pipe'), 'frames', 'heads'), parts along dimension 0, may hold values from -12 to 12
- key: bfloat16 [4, 1536, 3072], P(('groups', 'pipe'), 'frames', 'heads'), parts along dimension 0, may hold values from -6 to 6
- value: bfloat16 [4, 1536, 3072], P(('groups', 'pipe'), 'frames', 'heads'), parts along dimension 0, may hold values from -6 to 6
- stream: bfloat16 [4, 3072, 1536], P(('groups', 'pipe'), 'heads', 'frames'), parts along dimension 0, may hold values from -4 to 4
- w_out: bfloat16 [3072, 3072], P('heads'), may hold values from -0.109375 to 0.109375
- w_lat: bfloat16 [3072, 64], P('heads'), may hold values from -0.109375 to 0.109375
- latent: float32 [4, 64, 1536], P(('groups', 'pipe'), None, 'frames'), parts along dimension 0, may hold values from -6 to 6
- frame_clip: int32 [4, 12], P(('groups', 'pipe')), parts along dimension 0, may hold values from 0 to 2, never falling along the last dimension, each value on 1 to 6 neighbouring positions
- w_conv: bfloat16 [512, 432], P('heads'), may hold values from -0.3125 to 0.3125
- conv_bias: float32 [512], P('heads'), may hold values from -3 to 3
Outputs:
- hidden_out: bfloat16 [4, 3072, 1536], P(('groups', 'pipe'), 'heads', 'frames'), parts along dimension 0
- vae_feat: bfloat16 [4, 512, 12, 512], P(('groups', 'pipe'), 'heads', 'frames'), parts along dimension 0
The draws below stay inside these ranges and needn't reach their ends.
There are 2 independent parts, one for each index of `groups`. The reference program is written for one: setup_inputs(seed, part) draws one part's arguments, and reference() takes and returns one part's arrays. A program takes and returns all parts, laid end to end along the dimension named above; an argument that names none is the same for every part. Nothing has to cross between parts.
Inputs may be any that keep to these rules, and one draw needn't show every extreme that they name: In each row of frame_clip the clip numbers never fall, each of the 3 clips has 1 to 6 frames, and one has exactly 6.
All inputs are finite; a program needn't handle non-finite values.
Results may differ from the reference program's by a relative error of at most 0.0085.
Values may be sent and summed in bfloat16 or wider, within the bound.
A program may use at most 128 MiB of HBM per device.

```python
import math
import jax
import jax.numpy as jnp
import numpy as np
from jax import lax

HEADS = 24
HD = 128
D = 3072
LAT_CH = 16
LATP = 64
VAE_CH = 512
FH = 8
FW = 16
CLIPS = 3
SEQ_FR = 12
SEQ_TOK = 1536
SEQS = 2
PIX = 512
MAXCLIP = 6


def draw_query(key, part):
    drawn = jnp.clip(2.5 * jax.random.normal(jax.random.fold_in(key, 1), (SEQS, SEQ_TOK, D), jnp.float32), -12.0, 12.0)
    return drawn.astype(jnp.bfloat16)


def draw_key(key, part):
    drawn = jnp.clip(jax.random.normal(jax.random.fold_in(key, 2), (SEQS, SEQ_TOK, D), jnp.float32), -6.0, 6.0)
    return drawn.astype(jnp.bfloat16)


def shard_levels(stream_key, dims, cuts, low, top_value):
    def one(dim, blocks):
        draws = jax.random.uniform(jax.random.fold_in(jax.random.fold_in(stream_key, 6), dim), (blocks,), jnp.float32, low / len(cuts), top_value / len(cuts))
        return jnp.repeat(jnp.exp(draws), dims[dim] // blocks).reshape((-1,) + (1,) * (len(dims) - dim - 1))

    loudness = one(*cuts[0])
    for cut in cuts[1:]:
        loudness = loudness * one(*cut)
    return loudness


def length_profile(amount, total, reach, lean):
    weights = [(1 << 20) // math.isqrt(grade ** lean) + 1 for grade in range(2, amount + 1)]
    rest, given = total - reach - (amount - 1), [1] * (amount - 1)
    while rest > 0:
        movable = [i for i in range(amount - 1) if given[i] < reach]
        pool, budget = sum([weights[i] for i in movable]), rest
        for i in movable:
            addition = min(reach - given[i], max(1, budget * weights[i] // pool), rest)
            given[i] = given[i] + addition
            rest = rest - addition
    return np.array([reach] + given)


def ragged_sizes(stream_key, amount, total, bound, slope):
    if amount == 2:
        one = jax.random.randint(stream_key, (), max(1, total - bound), min(bound, total - 1) + 1)
        return jnp.stack([one, total - one])
    tallies = jnp.asarray(length_profile(amount, total, bound, slope), jnp.int32)
    twos = (amount - 1) // 2
    donor, receiver = tallies[1:1 + 2 * twos:2], tallies[2:2 + 2 * twos:2]
    margin = jnp.minimum(donor - 1, bound - receiver)
    moved = jax.random.randint(jax.random.fold_in(stream_key, 1), (twos,), 0, 1 << 20) % (margin + 1)
    tallies = tallies.at[1:1 + 2 * twos:2].set(donor - moved).at[2:2 + 2 * twos:2].set(receiver + moved)
    return tallies[jax.random.permutation(jax.random.fold_in(stream_key, 2), amount)]


def normal_values(stream_key, extent, scale, limit, shards=(), kind=jnp.bfloat16):
    level = shard_levels(stream_key, extent, shards, -0.22, 0.18) if shards else 1.0
    drawn = jax.random.normal(stream_key, extent, jnp.float32) * scale * level
    return jnp.minimum(jnp.maximum(drawn, -limit), limit).astype(kind)


def setup_inputs(seed: int = 0, part: int = 0) -> dict:
    key_of = jax.random.split(jax.random.key(seed), 11)
    own_keys = jax.random.split(jax.random.fold_in(key_of[10], part), 11)
    query = draw_query(jax.random.fold_in(jax.random.fold_in(key_of[10], part), 71), part)
    key = draw_key(jax.random.fold_in(jax.random.fold_in(key_of[10], part), 71), part)
    value = normal_values(own_keys[2], (SEQS, SEQ_TOK, D), 1.0, 6.0, ((0, 2), (1, 4), (2, 2)))
    stream = normal_values(own_keys[3], (SEQS, D, SEQ_TOK), 0.5, 4.0, ((0, 2), (1, 2), (2, 4)))
    w_out = normal_values(key_of[4], (D, D), D ** -0.5, 0.109375, ((0, 2),))
    w_lat = normal_values(key_of[5], (D, LATP), D ** -0.5, 0.109375, ((0, 2),))
    latent = normal_values(own_keys[6], (SEQS, LATP, SEQ_TOK), 1.0, 6.0, ((0, 2), (2, 4)), jnp.float32)
    frame_clip = jax.vmap(lambda own: jnp.searchsorted(jnp.cumsum(ragged_sizes(own, CLIPS, SEQ_FR, MAXCLIP, 0)), jnp.arange(SEQ_FR), side="right"))(jax.random.split(own_keys[7], SEQS)).reshape((SEQS, SEQ_FR)).astype(jnp.int32)
    w_conv = normal_values(key_of[8], (VAE_CH, 27 * LAT_CH), (27 * LAT_CH) ** -0.5, 0.3125, ((0, 2),))
    conv_bias = normal_values(key_of[9], (VAE_CH,), 0.5, 3.0, ((0, 2),), jnp.float32)
    return {"query": query, "key": key, "value": value, "stream": stream, "w_out": w_out, "w_lat": w_lat, "latent": latent, "frame_clip": frame_clip, "w_conv": w_conv, "conv_bias": conv_bias}


neg_fill = -1e+30
step_size = -0.5
highest = lax.Precision.HIGHEST

def unpatch(denoised, nframes):
    shaped = denoised.reshape(LAT_CH, 2, 2, nframes, FH, FW)
    shaped = jnp.transpose(shaped, (0, 3, 4, 1, 5, 2))
    return shaped.reshape(LAT_CH, nframes, 2 * FH, 2 * FW)

def clip_starts(clips):
    count = clips.shape[0]
    places = jnp.arange(count, dtype=jnp.int32)
    same = clips[:, None] == clips[None, :]
    return lax.optimization_barrier(jnp.min(jnp.where(same, places[None, :], count), axis=1)).astype(jnp.int32)

def reference(query, key, value, stream, w_out, w_lat, latent, frame_clip, w_conv, conv_bias):
    scale = 1.0 / math.sqrt(HD)
    frame_tok = FH * FW
    hidden_all = []
    feat_all = []
    for seq in range(SEQS):
        clips = frame_clip[seq]
        tok_clip = jnp.repeat(clips, frame_tok)
        visible = tok_clip[:, None] == tok_clip[None, :]
        q_heads = jnp.transpose(query[seq].reshape(SEQ_TOK, HEADS, HD), (1, 0, 2))
        k_heads = jnp.transpose(key[seq].reshape(SEQ_TOK, HEADS, HD), (1, 0, 2))
        v_heads = jnp.transpose(value[seq].reshape(SEQ_TOK, HEADS, HD), (1, 0, 2))

        def one_head(parts):
            q_one, k_one, v_one = parts
            scores = jnp.dot(q_one.astype(jnp.float32), k_one.astype(jnp.float32).T, precision=highest) * scale
            scores = jnp.where(visible, scores, neg_fill)
            row_max = lax.optimization_barrier(jnp.max(scores, axis=1))
            expo = jnp.where(visible, jnp.exp(scores - row_max[:, None]), 0.0)
            total = lax.optimization_barrier(jnp.sum(expo, axis=1))
            weights = expo.astype(jnp.bfloat16).astype(jnp.float32)
            summed = jnp.dot(weights, v_one.astype(jnp.float32), precision=highest)
            return (summed / total[:, None]).astype(jnp.bfloat16)
        heads_out = lax.map(one_head, (q_heads, k_heads, v_heads))
        attn = jnp.transpose(heads_out, (1, 0, 2)).reshape(SEQ_TOK, D)
        mixed = jnp.dot(attn.astype(jnp.float32), w_out.astype(jnp.float32), precision=highest).T
        hidden = (stream[seq].astype(jnp.float32) + mixed).astype(jnp.bfloat16)
        velocity = jnp.dot(w_lat.astype(jnp.float32).T, hidden.astype(jnp.float32), precision=highest)
        denoised = latent[seq] + step_size * velocity
        image = unpatch(denoised, SEQ_FR).astype(jnp.bfloat16)
        starts = clip_starts(clips)
        places = jnp.arange(SEQ_FR, dtype=jnp.int32)
        taps = jnp.arange(3, dtype=jnp.int32)
        source = jnp.maximum(places[:, None] - 2 + taps[None, :], starts[:, None]).astype(jnp.int32)
        chosen = jnp.take(image, source.reshape(-1), axis=1).reshape(LAT_CH, SEQ_FR, 3, 2 * FH, 2 * FW)
        chosen = jnp.transpose(chosen, (1, 2, 0, 3, 4))
        padded = jnp.pad(chosen, ((0, 0), (0, 0), (0, 0), (1, 1), (1, 1)))
        pieces = []
        for row_tap in range(3):
            for col_tap in range(3):
                pieces.append(padded[:, :, :, row_tap:row_tap + 2 * FH, col_tap:col_tap + 2 * FW])
        patches = jnp.stack(pieces, axis=2).reshape(SEQ_FR, 27 * LAT_CH, PIX)
        conv = jnp.einsum('ok,fkp->ofp', w_conv.astype(jnp.float32), patches.astype(jnp.float32), precision=highest)
        conv = conv + conv_bias[:, None, None]
        hidden_all.append(hidden)
        feat_all.append(conv.astype(jnp.bfloat16))
    return (jnp.stack(hidden_all, axis=0), jnp.stack(feat_all, axis=0))
```

```python
import functools
import math

import jax
import jax.numpy as jnp
from jax import lax
from jax.experimental import pallas as pl
from jax.experimental.pallas import tpu as pltpu
from jax.sharding import PartitionSpec as P

HD = 128
LAT_CH = 16
FH = 8
FW = 16
FT = FH * FW
CHUNK = 2
MESH = pl.DeviceIdType.MESH

neg_fill = -1e30
step_size = -0.5


def block_kernel(n, nh, np_, halo, fh, q_ref, k_hbm, v_hbm, bias_ref, stream_ref, w_hbm, wlat_ref, lat_ref,
                 hid_ref, den_ref,
                 kext, vext, attn, wmine, pvel, dext,
                 kv_send, kv_recv, at_send, at_recv, w_send, w_recv, s_send, s_recv, pv_send, pv_recv,
                 d_send, d_recv, loc):
    me = lax.axis_index("frames")
    hx = lax.axis_index("heads")
    px = lax.axis_index("pipe")
    tok, feats = q_ref.shape
    heads_here = feats // HD
    chunks = heads_here // CHUNK
    cw = CHUNK * HD
    hops = -(-halo // fh)
    model = w_hbm.shape[1]
    mcols = model // nh
    own0 = halo * FT
    has_right = me < n - 1
    has_left = me > 0
    sib = lax.rem(px + 1, np_)

    my_cols = pl.ds(pl.multiple_of(hx * mcols, 128), mcols)
    my_rows = pl.ds(pl.multiple_of(hx * feats, 128), feats)
    local = [
        pltpu.make_async_copy(k_hbm, kext.at[pl.ds(own0, tok)], loc.at[0]),
        pltpu.make_async_copy(v_hbm, vext.at[pl.ds(own0, tok)], loc.at[1]),
        pltpu.make_async_copy(w_hbm.at[:, my_cols], wmine.at[my_rows], loc.at[2]),
    ]
    for copy in local:
        copy.start()

    barrier = pltpu.get_barrier_semaphore()

    @pl.when(has_left)
    def _():
        pl.semaphore_signal(barrier, inc=1, device_id={"frames": me - 1}, device_id_type=MESH)

    @pl.when(has_right)
    def _():
        pl.semaphore_signal(barrier, inc=1, device_id={"frames": me + 1}, device_id_type=MESH)

    for step in range(1, nh):
        pl.semaphore_signal(barrier, inc=1, device_id={"heads": lax.rem(hx + step, nh)}, device_id_type=MESH)
    pl.semaphore_signal(barrier, inc=1, device_id={"pipe": sib}, device_id_type=MESH)
    pl.semaphore_wait(barrier, has_left.astype(jnp.int32) + has_right.astype(jnp.int32) + (nh - 1) + 1)

    def span(side, hop):
        if side == 0:
            low, high = max(0, halo - fh * hop), halo - fh * (hop - 1)
        else:
            low, high = halo + fh * hop, min(2 * halo + fh, halo + fh * (hop + 1))
        return low * FT, (high - low) * FT

    def kv_copies(side, hop, c):
        low, size = span(side, hop)
        cols = pl.ds(pl.multiple_of(c * cw, 128), cw)
        shift = fh * FT if side == 0 else -fh * FT
        made = []
        for which, (hbm, ext) in enumerate(((k_hbm, kext), (v_hbm, vext))):
            if hop == 1:
                src = hbm.at[pl.ds(low + shift - own0, size), cols]
            else:
                src = ext.at[pl.ds(low + shift, size), cols]
            made.append(pltpu.make_async_remote_copy(
                src_ref=src,
                dst_ref=ext.at[pl.ds(low, size), cols],
                send_sem=kv_send.at[side, hop - 1, c, which],
                recv_sem=kv_recv.at[side, hop - 1, c, which],
                device_id={"frames": me + 1 if side == 0 else me - 1},
                device_id_type=MESH,
            ))
        return made

    def sends(side, hop):
        if side == 0:
            return has_right & (me - (hop - 1) >= 0)
        return has_left & (me + (hop - 1) <= n - 1)

    def receives(side, hop):
        return me - hop >= 0 if side == 0 else me + hop <= n - 1

    def start_hop(hop, c):
        for side in range(2):
            @pl.when(sends(side, hop))
            def _():
                for copy in kv_copies(side, hop, c):
                    copy.start()

    def await_hop(hop, c):
        for side in range(2):
            @pl.when(receives(side, hop))
            def _():
                for copy in kv_copies(side, hop, c):
                    copy.wait_recv()

    half = feats // np_

    def w_copy(step):
        peer = lax.rem(hx + step, nh)
        return pltpu.make_async_remote_copy(
            src_ref=w_hbm.at[pl.ds(pl.multiple_of(px * half, 128), half),
                             pl.ds(pl.multiple_of(peer * mcols, 128), mcols)],
            dst_ref=wmine.at[pl.ds(pl.multiple_of(hx * feats + px * half, 128), half)],
            send_sem=w_send.at[step - 1], recv_sem=w_recv.at[step - 1],
            device_id={"heads": peer}, device_id_type=MESH)

    def sib_copy(step):
        origin = lax.rem(hx + nh - step, nh)
        rows = pl.ds(pl.multiple_of(origin * feats + px * half, 128), half)
        return pltpu.make_async_remote_copy(
            src_ref=wmine.at[rows], dst_ref=wmine.at[rows],
            send_sem=s_send.at[step - 1], recv_sem=s_recv.at[step - 1],
            device_id={"pipe": sib}, device_id_type=MESH)

    def at_copy(step, c):
        cols = pl.ds(pl.multiple_of(hx * feats + c * cw, 128), cw)
        return pltpu.make_async_remote_copy(
            src_ref=attn.at[:, cols], dst_ref=attn.at[:, cols],
            send_sem=at_send.at[step - 1, c], recv_sem=at_recv.at[step - 1, c],
            device_id={"heads": lax.rem(hx + step, nh)}, device_id_type=MESH)

    start_hop(1, 0)
    for step in range(1, nh):
        w_copy(step).start()

    for side in range(2):
        for hop in range(1, hops + 1):
            low, size = span(side, hop)

            @pl.when(jnp.logical_not(receives(side, hop)))
            def _():
                kext[pl.ds(low, size)] = jnp.zeros((size, feats), kext.dtype)
                vext[pl.ds(low, size)] = jnp.zeros((size, feats), vext.dtype)

    local[0].wait()
    local[1].wait()

    band = (2 * halo + 1) * FT
    factor = math.log2(math.e) / math.sqrt(HD)

    def head_step(c, inner):
        col = pl.multiple_of(c * cw + inner * HD, 128)
        cols = pl.ds(col, HD)
        for j in range(fh):
            rows = pl.ds(j * FT, FT)
            scores = lax.dot_general(
                q_ref[rows, cols], kext[pl.ds(j * FT, band), cols], (((1,), (1,)), ((), ())),
                preferred_element_type=jnp.float32)
            scores = scores + bias_ref[pl.ds(j, 1)]
            top = jnp.max(scores, axis=1, keepdims=True)
            expo = jnp.exp2((scores - top) * factor)
            total = jnp.sum(expo, axis=1, keepdims=True)
            summed = jnp.dot(expo.astype(jnp.bfloat16), vext[pl.ds(j * FT, band), cols],
                             preferred_element_type=jnp.float32)
            attn[rows, pl.ds(pl.multiple_of(hx * feats + col, 128), HD)] = (summed / total).astype(jnp.bfloat16)

    @pl.loop(0, chunks + hops)
    def _(t):
        @pl.when(t + 1 < chunks)
        def _():
            start_hop(1, t + 1)

        for hop in range(2, hops + 1):
            c = t - (hop - 2)

            @pl.when((c >= 0) & (c < chunks))
            def _():
                await_hop(hop - 1, c)
                start_hop(hop, c)

        done = t - hops

        @pl.when(done >= 0)
        def _():
            await_hop(hops, done)

            @pl.loop(0, CHUNK)
            def _(inner):
                head_step(done, inner)

            for step in range(1, nh):
                at_copy(step, done).start()

        @pl.when(t == chunks + hops - 2)
        def _():
            for step in range(1, nh):
                w_copy(step).wait_recv()
                sib_copy(step).start()

    for step in range(1, nh):
        sib_copy(step).wait_recv()
    local[2].wait()

    @pl.loop(0, chunks)
    def _(c):
        for step in range(1, nh):
            at_copy(step, c).wait_recv()

    mt = 256 if mcols % 256 == 0 else 128
    pvel[hx] = jnp.zeros(pvel.shape[1:], pvel.dtype)

    @pl.loop(0, mcols // mt)
    def _(i):
        rows = pl.ds(pl.multiple_of(i * mt, 128), mt)
        mixed = jnp.dot(attn[...], wmine[:, rows], preferred_element_type=jnp.float32)
        hidden = (stream_ref[rows].astype(jnp.float32) + mixed.T).astype(jnp.bfloat16)
        hid_ref[rows] = hidden
        pvel[hx] += lax.dot_general(wlat_ref[rows], hidden, (((0,), (0,)), ((), ())),
                                    preferred_element_type=jnp.float32)

    def pv_copy(step):
        return pltpu.make_async_remote_copy(
            src_ref=pvel.at[hx], dst_ref=pvel.at[hx],
            send_sem=pv_send.at[step - 1], recv_sem=pv_recv.at[step - 1],
            device_id={"heads": lax.rem(hx + step, nh)}, device_id_type=MESH)

    for step in range(1, nh):
        pv_copy(step).start()

    @pl.when(jnp.logical_not(has_left))
    def _():
        dext[:, pl.ds(0, 2 * FT)] = jnp.zeros((dext.shape[0], 2 * FT), dext.dtype)

    for step in range(1, nh):
        pv_copy(step).wait_recv()
    velocity = pvel[0]
    for p in range(1, nh):
        velocity = velocity + pvel[p]
    dext[:, pl.ds(2 * FT, tok)] = (lat_ref[...] + step_size * velocity).astype(jnp.bfloat16)
    last = pltpu.make_async_remote_copy(
        src_ref=dext.at[:, pl.ds(tok, 2 * FT)], dst_ref=dext.at[:, pl.ds(0, 2 * FT)],
        send_sem=d_send, recv_sem=d_recv, device_id={"frames": me + 1}, device_id_type=MESH)

    @pl.when(has_right)
    def _():
        last.start()

    @pl.loop(0, chunks)
    def _(c):
        for side in range(2):
            for hop in range(1, hops + 1):
                @pl.when(sends(side, hop))
                def _():
                    for copy in kv_copies(side, hop, c):
                        copy.wait_send()
        for step in range(1, nh):
            at_copy(step, c).wait_send()

    for step in range(1, nh):
        w_copy(step).wait_send()
        sib_copy(step).wait_send()
        pv_copy(step).wait_send()

    @pl.when(has_left)
    def _():
        last.wait_recv()

    den_ref[...] = dext[...]

    @pl.when(has_right)
    def _():
        last.wait_send()


def conv_kernel(fh, src_ref, den_ref, w_ref, bias_ref, out_ref, patch):
    pix = 4 * FT
    row64 = lax.broadcasted_iota(jnp.int32, (LAT_CH, 4 * LAT_CH), 1)
    ch = lax.broadcasted_iota(jnp.int32, (LAT_CH, 4 * LAT_CH), 0)
    tokn = lax.broadcasted_iota(jnp.int32, (FT, pix), 0)
    where = lax.broadcasted_iota(jnp.int32, (FT, pix), 1)
    lane = lax.broadcasted_iota(jnp.int32, (LAT_CH, pix), 1)
    width = 2 * FW
    ypos, xpos = lane // width, lane % width
    selects, places = [], []
    for phase in range(4):
        p, q = phase // 2, phase % 2
        selects.append((row64 == 4 * ch + phase).astype(jnp.bfloat16))
        target = (2 * (tokn // FW) + p) * width + 2 * (tokn % FW) + q
        places.append((where == target).astype(jnp.bfloat16))
    for e in range(fh + 2):
        frame = den_ref[:, pl.ds(e * FT, FT)]
        image = jnp.zeros((LAT_CH, pix), jnp.float32)
        for phase in range(4):
            rows = jnp.dot(selects[phase], frame, preferred_element_type=jnp.float32).astype(jnp.bfloat16)
            image = image + jnp.dot(rows, places[phase], preferred_element_type=jnp.float32)
        for i in range(3):
            for j in range(3):
                shift = (i - 1) * width + (j - 1)
                moved = pltpu.roll(image, (-shift) % pix, 1) if shift else image
                ok = ((ypos + (i - 1) >= 0) & (ypos + (i - 1) < 2 * FH)
                      & (xpos + (j - 1) >= 0) & (xpos + (j - 1) < width))
                patch[e, pl.ds((3 * i + j) * LAT_CH, LAT_CH)] = jnp.where(ok, moved, 0.0).astype(jnp.bfloat16)
    part = 9 * LAT_CH
    for f in range(fh):
        rows = jnp.concatenate([patch[src_ref[3 * f + k]] for k in range(3)], axis=0)
        conv = jnp.dot(w_ref[...], rows, preferred_element_type=jnp.float32)
        out_ref[:, f, :] = (conv + bias_ref[...]).astype(jnp.bfloat16)


def shards(n, nh, np_, query, key, value, stream, w_out, w_lat, latent, frame_clip, w_conv, conv_bias):
    tok, feats = query.shape[1:]
    fh = tok // FT
    clips = frame_clip[0]
    seq_frames = clips.shape[0]
    halo = seq_frames // 2 - 1
    hops = -(-halo // fh)
    chunks = feats // HD // CHUNK
    first = lax.axis_index("frames") * fh
    padded = jnp.concatenate([jnp.full((halo,), -1, jnp.int32), clips, jnp.full((halo,), -1, jnp.int32)])
    near = lax.dynamic_slice_in_dim(padded, first, 2 * halo + fh)
    mine = near[halo:halo + fh]
    bands = jnp.stack([near[j:j + 2 * halo + 1] for j in range(fh)])
    bias = jnp.where(bands == mine[:, None], 0.0, neg_fill).astype(jnp.float32)
    bias = jnp.repeat(bias, FT, axis=1)
    model, mcols = w_out.shape[1], stream.shape[1]
    latp = w_lat.shape[1]
    ext = (2 * halo + fh) * FT
    vmem = pl.BlockSpec(memory_space=pltpu.VMEM)
    hbm = pl.BlockSpec(memory_space=pl.ANY)
    peers = max(1, nh - 1)
    dma = pltpu.SemaphoreType.DMA
    hidden, den = pl.pallas_call(
        functools.partial(block_kernel, n, nh, np_, halo, fh),
        out_shape=(jax.ShapeDtypeStruct((mcols, tok), jnp.bfloat16),
                   jax.ShapeDtypeStruct((latp, tok + 2 * FT), jnp.bfloat16)),
        in_specs=[vmem, hbm, hbm, vmem, vmem, hbm, vmem, vmem],
        out_specs=(vmem, vmem),
        scratch_shapes=[
            pltpu.VMEM((ext, feats), jnp.bfloat16),
            pltpu.VMEM((ext, feats), jnp.bfloat16),
            pltpu.VMEM((tok, nh * feats), jnp.bfloat16),
            pltpu.VMEM((nh * feats, mcols), jnp.bfloat16),
            pltpu.VMEM((nh, latp, tok), jnp.float32),
            pltpu.VMEM((latp, tok + 2 * FT), jnp.bfloat16),
            dma((2, hops, chunks, 2)), dma((2, hops, chunks, 2)),
            dma((peers, chunks)), dma((peers, chunks)),
            dma((peers,)), dma((peers,)),
            dma((peers,)), dma((peers,)),
            dma((peers,)), dma((peers,)),
            dma(()), dma(()), dma((3,)),
        ],
        compiler_params=pltpu.CompilerParams(collective_id=0, has_side_effects=True,
                                             vmem_limit_bytes=56 * 1024 * 1024),
        name="clip_block",
    )(query[0], key[0], value[0], bias, stream[0], w_out, w_lat, latent[0])

    places = jnp.arange(seq_frames, dtype=jnp.int32)
    same_clip = clips[:, None] == clips[None, :]
    starts = jnp.min(jnp.where(same_clip, places[None, :], seq_frames), axis=1)
    my_starts = lax.dynamic_slice_in_dim(starts, first, fh)
    mine_at = first + jnp.arange(fh, dtype=jnp.int32)
    taps = jnp.arange(3, dtype=jnp.int32)
    source = jnp.maximum(mine_at[:, None] - 2 + taps[None, :], my_starts[:, None]) - (first - 2)
    outs = w_conv.shape[0]
    feat = pl.pallas_call(
        functools.partial(conv_kernel, fh),
        out_shape=jax.ShapeDtypeStruct((outs, fh, 4 * FT), jnp.bfloat16),
        in_specs=[pl.BlockSpec(memory_space=pltpu.SMEM), vmem, vmem, vmem],
        out_specs=vmem,
        scratch_shapes=[pltpu.VMEM((fh + 2, 9 * LAT_CH, 4 * FT), jnp.bfloat16)],
        name="causal_conv",
    )(source.reshape(-1), den, w_conv, conv_bias[:, None])
    return (hidden[None], feat[None])


def solution(mesh):
    sizes = dict(mesh.shape)
    return jax.shard_map(
        functools.partial(shards, sizes["frames"], sizes["heads"], sizes["pipe"]),
        mesh=mesh,
        in_specs=(
            P(("groups", "pipe"), "frames", "heads"),
            P(("groups", "pipe"), "frames", "heads"),
            P(("groups", "pipe"), "frames", "heads"),
            P(("groups", "pipe"), "heads", "frames"),
            P("heads", None),
            P("heads", None),
            P(("groups", "pipe"), None, "frames"),
            P(("groups", "pipe"), None),
            P("heads", None),
            P("heads"),
        ),
        out_specs=(
            P(("groups", "pipe"), "heads", "frames"),
            P(("groups", "pipe"), "heads", "frames", None),
        ),
        check_vma=False,
    )
```

```python
import functools
import math

import jax
import jax.numpy as jnp
from jax import lax
from jax.experimental import pallas as pl
from jax.experimental.pallas import tpu as pltpu
from jax.sharding import PartitionSpec as P

HD = 128
LAT_CH = 16
FH = 8
FW = 16
FT = FH * FW
CHUNK = 1
MESH = pl.DeviceIdType.MESH

neg_fill = -1e30
step_size = -0.5


def block_kernel(n, nh, np_, halo, fh, clip_ref, q_ref, k_hbm, v_hbm, stream_ref, w_hbm, wlat_ref, lat_ref,
                 hid_ref, den_ref,
                 bias_ref, kext, vext, attn, wmine, pvel, dext,
                 kv_send, kv_recv, at_send, at_recv, w_send, w_recv, s_send, s_recv, pv_send, pv_recv,
                 d_send, d_recv, loc):
    me = lax.axis_index("frames")
    hx = lax.axis_index("heads")
    px = lax.axis_index("pipe")
    tok, feats = q_ref.shape
    heads_here = feats // HD
    chunks = heads_here // CHUNK
    cw = CHUNK * HD
    hops = -(-halo // fh)
    model = w_hbm.shape[1]
    mcols = model // nh
    own0 = halo * FT
    has_right = me < n - 1
    has_left = me > 0
    sib = lax.rem(px + 1, np_)

    my_cols = pl.ds(pl.multiple_of(hx * mcols, 128), mcols)
    my_rows = pl.ds(pl.multiple_of(hx * feats, 128), feats)
    local = [
        pltpu.make_async_copy(k_hbm, kext.at[pl.ds(own0, tok)], loc.at[0]),
        pltpu.make_async_copy(v_hbm, vext.at[pl.ds(own0, tok)], loc.at[1]),
        pltpu.make_async_copy(w_hbm.at[:, my_cols], wmine.at[my_rows], loc.at[2]),
    ]
    for copy in local:
        copy.start()

    barrier = pltpu.get_barrier_semaphore()

    @pl.when(has_left)
    def _():
        pl.semaphore_signal(barrier, inc=1, device_id={"frames": me - 1}, device_id_type=MESH)

    @pl.when(has_right)
    def _():
        pl.semaphore_signal(barrier, inc=1, device_id={"frames": me + 1}, device_id_type=MESH)

    for step in range(1, nh):
        pl.semaphore_signal(barrier, inc=1, device_id={"heads": lax.rem(hx + step, nh)}, device_id_type=MESH)
    pl.semaphore_signal(barrier, inc=1, device_id={"pipe": sib}, device_id_type=MESH)
    pl.semaphore_wait(barrier, has_left.astype(jnp.int32) + has_right.astype(jnp.int32) + (nh - 1) + 1)

    def span(side, hop):
        if side == 0:
            low, high = max(0, halo - fh * hop), halo - fh * (hop - 1)
        else:
            low, high = halo + fh * hop, min(2 * halo + fh, halo + fh * (hop + 1))
        return low * FT, (high - low) * FT

    def kv_copies(side, hop, c):
        low, size = span(side, hop)
        cols = pl.ds(pl.multiple_of(c * cw, 128), cw)
        shift = fh * FT if side == 0 else -fh * FT
        made = []
        for which, (hbm, ext) in enumerate(((k_hbm, kext), (v_hbm, vext))):
            if hop == 1:
                src = hbm.at[pl.ds(low + shift - own0, size), cols]
            else:
                src = ext.at[pl.ds(low + shift, size), cols]
            made.append(pltpu.make_async_remote_copy(
                src_ref=src,
                dst_ref=ext.at[pl.ds(low, size), cols],
                send_sem=kv_send.at[side, hop - 1, c, which],
                recv_sem=kv_recv.at[side, hop - 1, c, which],
                device_id={"frames": me + 1 if side == 0 else me - 1},
                device_id_type=MESH,
            ))
        return made

    def sends(side, hop):
        if side == 0:
            return has_right & (me - (hop - 1) >= 0)
        return has_left & (me + (hop - 1) <= n - 1)

    def receives(side, hop):
        return me - hop >= 0 if side == 0 else me + hop <= n - 1

    def start_hop(hop, c):
        for side in range(2):
            @pl.when(sends(side, hop))
            def _():
                for copy in kv_copies(side, hop, c):
                    copy.start()

    def await_hop(hop, c):
        for side in range(2):
            @pl.when(receives(side, hop))
            def _():
                for copy in kv_copies(side, hop, c):
                    copy.wait_recv()

    half = feats // np_

    def w_copy(step):
        peer = lax.rem(hx + step, nh)
        return pltpu.make_async_remote_copy(
            src_ref=w_hbm.at[pl.ds(pl.multiple_of(px * half, 128), half),
                             pl.ds(pl.multiple_of(peer * mcols, 128), mcols)],
            dst_ref=wmine.at[pl.ds(pl.multiple_of(hx * feats + px * half, 128), half)],
            send_sem=w_send.at[step - 1], recv_sem=w_recv.at[step - 1],
            device_id={"heads": peer}, device_id_type=MESH)

    def sib_copy(step):
        origin = lax.rem(hx + nh - step, nh)
        rows = pl.ds(pl.multiple_of(origin * feats + px * half, 128), half)
        return pltpu.make_async_remote_copy(
            src_ref=wmine.at[rows], dst_ref=wmine.at[rows],
            send_sem=s_send.at[step - 1], recv_sem=s_recv.at[step - 1],
            device_id={"pipe": sib}, device_id_type=MESH)

    def at_copy(step, c):
        cols = pl.ds(pl.multiple_of(hx * feats + c * cw, 128), cw)
        return pltpu.make_async_remote_copy(
            src_ref=attn.at[:, cols], dst_ref=attn.at[:, cols],
            send_sem=at_send.at[step - 1, c], recv_sem=at_recv.at[step - 1, c],
            device_id={"heads": lax.rem(hx + step, nh)}, device_id_type=MESH)

    start_hop(1, 0)
    for step in range(1, nh):
        w_copy(step).start()

    for side in range(2):
        for hop in range(1, hops + 1):
            low, size = span(side, hop)

            @pl.when(jnp.logical_not(receives(side, hop)))
            def _():
                kext[pl.ds(low, size)] = jnp.zeros((size, feats), kext.dtype)
                vext[pl.ds(low, size)] = jnp.zeros((size, feats), vext.dtype)

    seq_frames = clip_ref.shape[1]
    first = me * fh
    for j in range(fh):
        for e in range(2 * halo + 1):
            g = first + j + e - halo
            seen = clip_ref[0, jnp.clip(g, 0, seq_frames - 1)] == clip_ref[0, first + j]
            seen = seen & (g >= 0) & (g < seq_frames)
            bias_ref[pl.ds(j, 1), pl.ds(e * FT, FT)] = jnp.full(
                (1, FT), jnp.where(seen, 0.0, neg_fill), jnp.float32)

    local[0].wait()
    local[1].wait()

    band = (2 * halo + 1) * FT
    factor = math.log2(math.e) / math.sqrt(HD)

    def head_step(c, inner):
        col = pl.multiple_of(c * cw + inner * HD, 128)
        cols = pl.ds(col, HD)
        for j in range(fh):
            rows = pl.ds(j * FT, FT)
            scores = lax.dot_general(
                q_ref[rows, cols], kext[pl.ds(j * FT, band), cols], (((1,), (1,)), ((), ())),
                preferred_element_type=jnp.float32)
            scores = scores + bias_ref[pl.ds(j, 1)]
            top = jnp.max(scores, axis=1, keepdims=True)
            expo = jnp.exp2((scores - top) * factor)
            total = jnp.sum(expo, axis=1, keepdims=True)
            summed = jnp.dot(expo.astype(jnp.bfloat16), vext[pl.ds(j * FT, band), cols],
                             preferred_element_type=jnp.float32)
            attn[rows, pl.ds(pl.multiple_of(hx * feats + col, 128), HD)] = (summed / total).astype(jnp.bfloat16)

    @pl.loop(0, chunks + hops)
    def _(t):
        @pl.when(t + 1 < chunks)
        def _():
            start_hop(1, t + 1)

        for hop in range(2, hops + 1):
            c = t - (hop - 2)

            @pl.when((c >= 0) & (c < chunks))
            def _():
                await_hop(hop - 1, c)
                start_hop(hop, c)

        done = t - hops

        @pl.when(done >= 0)
        def _():
            await_hop(hops, done)

            @pl.loop(0, CHUNK)
            def _(inner):
                head_step(done, inner)

            for step in range(1, nh):
                at_copy(step, done).start()

        @pl.when(t == chunks + hops - 2)
        def _():
            for step in range(1, nh):
                w_copy(step).wait_recv()
                sib_copy(step).start()

    for step in range(1, nh):
        sib_copy(step).wait_recv()
    local[2].wait()

    @pl.loop(0, chunks)
    def _(c):
        for step in range(1, nh):
            at_copy(step, c).wait_recv()

    mt = 256 if mcols % 256 == 0 else 128
    pvel[hx] = jnp.zeros(pvel.shape[1:], pvel.dtype)

    @pl.loop(0, mcols // mt)
    def _(i):
        rows = pl.ds(pl.multiple_of(i * mt, 128), mt)
        mixed = jnp.dot(attn[...], wmine[:, rows], preferred_element_type=jnp.float32)
        hidden = (stream_ref[rows].astype(jnp.float32) + mixed.T).astype(jnp.bfloat16)
        hid_ref[rows] = hidden
        pvel[hx] += jnp.dot(wlat_ref[:, rows], hidden, preferred_element_type=jnp.float32)

    def pv_copy(step):
        return pltpu.make_async_remote_copy(
            src_ref=pvel.at[hx], dst_ref=pvel.at[hx],
            send_sem=pv_send.at[step - 1], recv_sem=pv_recv.at[step - 1],
            device_id={"heads": lax.rem(hx + step, nh)}, device_id_type=MESH)

    for step in range(1, nh):
        pv_copy(step).start()

    @pl.when(jnp.logical_not(has_left))
    def _():
        dext[:, pl.ds(0, 2 * FT)] = jnp.zeros((dext.shape[0], 2 * FT), dext.dtype)

    for step in range(1, nh):
        pv_copy(step).wait_recv()
    velocity = pvel[0]
    for p in range(1, nh):
        velocity = velocity + pvel[p]
    dext[:, pl.ds(2 * FT, tok)] = (lat_ref[...] + step_size * velocity).astype(jnp.bfloat16)
    last = pltpu.make_async_remote_copy(
        src_ref=dext.at[:, pl.ds(tok, 2 * FT)], dst_ref=dext.at[:, pl.ds(0, 2 * FT)],
        send_sem=d_send, recv_sem=d_recv, device_id={"frames": me + 1}, device_id_type=MESH)

    @pl.when(has_right)
    def _():
        last.start()

    @pl.loop(0, chunks)
    def _(c):
        for side in range(2):
            for hop in range(1, hops + 1):
                @pl.when(sends(side, hop))
                def _():
                    for copy in kv_copies(side, hop, c):
                        copy.wait_send()
        for step in range(1, nh):
            at_copy(step, c).wait_send()

    for step in range(1, nh):
        w_copy(step).wait_send()
        sib_copy(step).wait_send()
        pv_copy(step).wait_send()

    @pl.when(has_left)
    def _():
        last.wait_recv()

    den_ref[...] = dext[...]

    @pl.when(has_right)
    def _():
        last.wait_send()


def conv_kernel(fh, clip_ref, den_ref, w_ref, bias_ref, hid_ref, out_ref, hid_out, patch, sem):
    moved_hidden = pltpu.make_async_copy(hid_ref, hid_out, sem)
    moved_hidden.start()
    first = lax.axis_index("frames") * fh
    pix = 4 * FT
    row64 = lax.broadcasted_iota(jnp.int32, (LAT_CH, 4 * LAT_CH), 1)
    ch = lax.broadcasted_iota(jnp.int32, (LAT_CH, 4 * LAT_CH), 0)
    tokn = lax.broadcasted_iota(jnp.int32, (FT, pix), 0)
    where = lax.broadcasted_iota(jnp.int32, (FT, pix), 1)
    lane = lax.broadcasted_iota(jnp.int32, (LAT_CH, pix), 1)
    width = 2 * FW
    ypos, xpos = lane // width, lane % width
    selects, places = [], []
    for phase in range(4):
        p, q = phase // 2, phase % 2
        selects.append((row64 == 4 * ch + phase).astype(jnp.bfloat16))
        target = (2 * (tokn // FW) + p) * width + 2 * (tokn % FW) + q
        places.append((where == target).astype(jnp.bfloat16))
    for e in range(fh + 2):
        frame = den_ref[:, pl.ds(e * FT, FT)]
        image = jnp.zeros((LAT_CH, pix), jnp.float32)
        for phase in range(4):
            rows = jnp.dot(selects[phase], frame, preferred_element_type=jnp.float32).astype(jnp.bfloat16)
            image = image + jnp.dot(rows, places[phase], preferred_element_type=jnp.float32)
        for i in range(3):
            for j in range(3):
                shift = (i - 1) * width + (j - 1)
                moved = pltpu.roll(image, (-shift) % pix, 1) if shift else image
                ok = ((ypos + (i - 1) >= 0) & (ypos + (i - 1) < 2 * FH)
                      & (xpos + (j - 1) >= 0) & (xpos + (j - 1) < width))
                patch[e, pl.ds((3 * i + j) * LAT_CH, LAT_CH)] = jnp.where(ok, moved, 0.0).astype(jnp.bfloat16)
    bias = bias_ref[...].T
    for f in range(fh):
        here = clip_ref[0, first + f]
        back1 = jnp.where((first + f >= 1) & (clip_ref[0, jnp.maximum(first + f - 1, 0)] == here), 1, 0)
        back2 = jnp.where((first + f >= 2) & (clip_ref[0, jnp.maximum(first + f - 2, 0)] == here), 2, back1)
        rows = jnp.concatenate([patch[f + 2 - back2], patch[f + 2 - back1], patch[f + 2]], axis=0)
        conv = lax.dot_general(w_ref[...], rows, (((0,), (0,)), ((), ())), preferred_element_type=jnp.float32)
        out_ref[f] = (conv + bias).astype(jnp.bfloat16)
    moved_hidden.wait()


def shards(n, nh, np_, query, key, value, stream, w_out, w_lat, latent, frame_clip, w_conv, conv_bias):
    tok, feats = query.shape[1:]
    fh = tok // FT
    seq_frames = frame_clip.shape[1]
    halo = seq_frames // 2 - 1
    hops = -(-halo // fh)
    chunks = feats // HD // CHUNK
    model, mcols = w_out.shape[1], stream.shape[1]
    latp = w_lat.shape[1]
    ext = (2 * halo + fh) * FT
    vmem = pl.BlockSpec(memory_space=pltpu.VMEM)
    hbm = pl.BlockSpec(memory_space=pl.ANY)
    smem = pl.BlockSpec(memory_space=pltpu.SMEM)
    peers = max(1, nh - 1)
    dma = pltpu.SemaphoreType.DMA
    hidden, den = pl.pallas_call(
        functools.partial(block_kernel, n, nh, np_, halo, fh),
        out_shape=(jax.ShapeDtypeStruct((mcols, tok), jnp.bfloat16),
                   jax.ShapeDtypeStruct((latp, tok + 2 * FT), jnp.bfloat16)),
        in_specs=[smem, vmem, hbm, hbm, vmem, hbm, vmem, vmem],
        out_specs=(vmem, vmem),
        scratch_shapes=[
            pltpu.VMEM((fh, (2 * halo + 1) * FT), jnp.float32),
            pltpu.VMEM((ext, feats), jnp.bfloat16),
            pltpu.VMEM((ext, feats), jnp.bfloat16),
            pltpu.VMEM((tok, nh * feats), jnp.bfloat16),
            pltpu.VMEM((nh * feats, mcols), jnp.bfloat16),
            pltpu.VMEM((nh, latp, tok), jnp.float32),
            pltpu.VMEM((latp, tok + 2 * FT), jnp.bfloat16),
            dma((2, hops, chunks, 2)), dma((2, hops, chunks, 2)),
            dma((peers, chunks)), dma((peers, chunks)),
            dma((peers,)), dma((peers,)),
            dma((peers,)), dma((peers,)),
            dma((peers,)), dma((peers,)),
            dma(()), dma(()), dma((3,)),
        ],
        compiler_params=pltpu.CompilerParams(collective_id=0, has_side_effects=True,
                                             vmem_limit_bytes=56 * 1024 * 1024),
        name="clip_block",
    )(frame_clip, query[0], key[0], value[0], stream[0], w_out, w_lat.T, latent[0])

    outs = w_conv.shape[0]
    feat, hidden = pl.pallas_call(
        functools.partial(conv_kernel, fh),
        out_shape=(jax.ShapeDtypeStruct((fh, outs, 4 * FT), jnp.bfloat16),
                   jax.ShapeDtypeStruct((mcols, tok), jnp.bfloat16)),
        in_specs=[smem, vmem, vmem, vmem, hbm],
        out_specs=(vmem, hbm),
        scratch_shapes=[pltpu.VMEM((fh + 2, 9 * LAT_CH, 4 * FT), jnp.bfloat16), dma(())],
        name="causal_conv",
    )(frame_clip, den, w_conv.T, conv_bias[None, :], hidden)
    return (hidden[None], jnp.transpose(feat, (1, 0, 2))[None])


def solution(mesh):
    sizes = dict(mesh.shape)
    return jax.shard_map(
        functools.partial(shards, sizes["frames"], sizes["heads"], sizes["pipe"]),
        mesh=mesh,
        in_specs=(
            P(("groups", "pipe"), "frames", "heads"),
            P(("groups", "pipe"), "frames", "heads"),
            P(("groups", "pipe"), "frames", "heads"),
            P(("groups", "pipe"), "heads", "frames"),
            P("heads", None),
            P("heads", None),
            P(("groups", "pipe"), None, "frames"),
            P(("groups", "pipe"), None),
            P("heads", None),
            P("heads"),
        ),
        out_specs=(
            P(("groups", "pipe"), "heads", "frames"),
            P(("groups", "pipe"), "heads", "frames", None),
        ),
        check_vma=False,
    )
```

```python
import functools
import math

import jax
import jax.numpy as jnp
from jax import lax
from jax.experimental import pallas as pl
from jax.experimental.pallas import tpu as pltpu
from jax.sharding import PartitionSpec as P

HD = 128
LAT_CH = 16
FH = 8
FW = 16
FT = FH * FW
CHUNK = 1
AHEAD = 2
LAG = AHEAD + 1
MESH = pl.DeviceIdType.MESH

neg_fill = -1e30
step_size = -0.5


def block_kernel(n, nh, np_, halo, fh, clip_ref, q_ref, k_hbm, v_hbm, stream_ref, w_hbm, wlat_ref, lat_ref,
                 hid_ref, den_ref,
                 bias_ref, kext, vext, attn, wmine, pvel, dext,
                 kv_send, kv_recv, at_send, at_recv, w_send, w_recv, s_send, s_recv, pv_send, pv_recv,
                 d_send, d_recv, loc):
    me = lax.axis_index("frames")
    hx = lax.axis_index("heads")
    px = lax.axis_index("pipe")
    tok, feats = q_ref.shape
    heads_here = feats // HD
    chunks = heads_here // CHUNK
    cw = CHUNK * HD
    hops = -(-halo // fh)
    model = w_hbm.shape[1]
    mcols = model // nh
    own0 = halo * FT
    has_right = me < n - 1
    has_left = me > 0
    sib = lax.rem(px + 1, np_)

    my_cols = pl.ds(pl.multiple_of(hx * mcols, 128), mcols)
    my_rows = pl.ds(pl.multiple_of(hx * feats, 128), feats)
    local = [
        pltpu.make_async_copy(k_hbm, kext.at[pl.ds(own0, tok)], loc.at[0]),
        pltpu.make_async_copy(v_hbm, vext.at[pl.ds(own0, tok)], loc.at[1]),
        pltpu.make_async_copy(w_hbm.at[:, my_cols], wmine.at[my_rows], loc.at[2]),
    ]
    for copy in local:
        copy.start()

    barrier = pltpu.get_barrier_semaphore()

    @pl.when(has_left)
    def _():
        pl.semaphore_signal(barrier, inc=1, device_id={"frames": me - 1}, device_id_type=MESH)

    @pl.when(has_right)
    def _():
        pl.semaphore_signal(barrier, inc=1, device_id={"frames": me + 1}, device_id_type=MESH)

    for step in range(1, nh):
        pl.semaphore_signal(barrier, inc=1, device_id={"heads": lax.rem(hx + step, nh)}, device_id_type=MESH)
    pl.semaphore_signal(barrier, inc=1, device_id={"pipe": sib}, device_id_type=MESH)
    pl.semaphore_wait(barrier, has_left.astype(jnp.int32) + has_right.astype(jnp.int32) + (nh - 1) + 1)

    def span(side, hop):
        if side == 0:
            low, high = max(0, halo - fh * hop), halo - fh * (hop - 1)
        else:
            low, high = halo + fh * hop, min(2 * halo + fh, halo + fh * (hop + 1))
        return low * FT, (high - low) * FT

    def kv_copies(side, hop, c):
        low, size = span(side, hop)
        cols = pl.ds(pl.multiple_of(c * cw, 128), cw)
        shift = fh * FT if side == 0 else -fh * FT
        made = []
        for which, (hbm, ext) in enumerate(((k_hbm, kext), (v_hbm, vext))):
            if hop == 1:
                src = hbm.at[pl.ds(low + shift - own0, size), cols]
            else:
                src = ext.at[pl.ds(low + shift, size), cols]
            made.append(pltpu.make_async_remote_copy(
                src_ref=src,
                dst_ref=ext.at[pl.ds(low, size), cols],
                send_sem=kv_send.at[side, hop - 1, c, which],
                recv_sem=kv_recv.at[side, hop - 1, c, which],
                device_id={"frames": me + 1 if side == 0 else me - 1},
                device_id_type=MESH,
            ))
        return made

    def sends(side, hop):
        if side == 0:
            return has_right & (me - (hop - 1) >= 0)
        return has_left & (me + (hop - 1) <= n - 1)

    def receives(side, hop):
        return me - hop >= 0 if side == 0 else me + hop <= n - 1

    def start_hop(hop, c):
        for side in range(2):
            @pl.when(sends(side, hop))
            def _():
                for copy in kv_copies(side, hop, c):
                    copy.start()

    def await_hop(hop, c):
        for side in range(2):
            @pl.when(receives(side, hop))
            def _():
                for copy in kv_copies(side, hop, c):
                    copy.wait_recv()

    half = feats // np_

    def w_copy(step):
        peer = lax.rem(hx + step, nh)
        return pltpu.make_async_remote_copy(
            src_ref=w_hbm.at[pl.ds(pl.multiple_of(px * half, 128), half),
                             pl.ds(pl.multiple_of(peer * mcols, 128), mcols)],
            dst_ref=wmine.at[pl.ds(pl.multiple_of(hx * feats + px * half, 128), half)],
            send_sem=w_send.at[step - 1], recv_sem=w_recv.at[step - 1],
            device_id={"heads": peer}, device_id_type=MESH)

    def sib_copy(step):
        origin = lax.rem(hx + nh - step, nh)
        rows = pl.ds(pl.multiple_of(origin * feats + px * half, 128), half)
        return pltpu.make_async_remote_copy(
            src_ref=wmine.at[rows], dst_ref=wmine.at[rows],
            send_sem=s_send.at[step - 1], recv_sem=s_recv.at[step - 1],
            device_id={"pipe": sib}, device_id_type=MESH)

    def at_copy(step, c):
        cols = pl.ds(pl.multiple_of(hx * feats + c * cw, 128), cw)
        return pltpu.make_async_remote_copy(
            src_ref=attn.at[:, cols], dst_ref=attn.at[:, cols],
            send_sem=at_send.at[step - 1, c], recv_sem=at_recv.at[step - 1, c],
            device_id={"heads": lax.rem(hx + step, nh)}, device_id_type=MESH)

    start_hop(1, 0)
    for step in range(1, nh):
        w_copy(step).start()

    for side in range(2):
        for hop in range(1, hops + 1):
            low, size = span(side, hop)

            @pl.when(jnp.logical_not(receives(side, hop)))
            def _():
                kext[pl.ds(low, size)] = jnp.zeros((size, feats), kext.dtype)
                vext[pl.ds(low, size)] = jnp.zeros((size, feats), vext.dtype)

    seq_frames = clip_ref.shape[1]
    first = me * fh
    for j in range(fh):
        for e in range(2 * halo + 1):
            g = first + j + e - halo
            seen = clip_ref[0, jnp.clip(g, 0, seq_frames - 1)] == clip_ref[0, first + j]
            seen = seen & (g >= 0) & (g < seq_frames)
            bias_ref[pl.ds(j, 1), pl.ds(e * FT, FT)] = jnp.full(
                (1, FT), jnp.where(seen, 0.0, neg_fill), jnp.float32)

    local[0].wait()
    local[1].wait()

    band = (2 * halo + 1) * FT
    factor = math.log2(math.e) / math.sqrt(HD)

    def head_step(c, inner):
        col = pl.multiple_of(c * cw + inner * HD, 128)
        cols = pl.ds(col, HD)
        for j in range(fh):
            rows = pl.ds(j * FT, FT)
            scores = lax.dot_general(
                q_ref[rows, cols], kext[pl.ds(j * FT, band), cols], (((1,), (1,)), ((), ())),
                preferred_element_type=jnp.float32)
            scores = scores + bias_ref[pl.ds(j, 1)]
            top = jnp.max(scores, axis=1, keepdims=True)
            expo = jnp.exp2((scores - top) * factor)
            total = jnp.sum(expo, axis=1, keepdims=True)
            summed = jnp.dot(expo.astype(jnp.bfloat16), vext[pl.ds(j * FT, band), cols],
                             preferred_element_type=jnp.float32)
            attn[rows, pl.ds(pl.multiple_of(hx * feats + col, 128), HD)] = (summed / total).astype(jnp.bfloat16)

    @pl.loop(0, chunks + hops)
    def _(t):
        @pl.when(t + 1 < chunks)
        def _():
            start_hop(1, t + 1)

        for hop in range(2, hops + 1):
            c = t - (hop - 2)

            @pl.when((c >= 0) & (c < chunks))
            def _():
                await_hop(hop - 1, c)
                start_hop(hop, c)

        done = t - hops

        @pl.when(done >= 0)
        def _():
            await_hop(hops, done)

            @pl.loop(0, CHUNK)
            def _(inner):
                head_step(done, inner)

            for step in range(1, nh):
                at_copy(step, done).start()

        @pl.when(t == chunks + hops - 2)
        def _():
            for step in range(1, nh):
                w_copy(step).wait_recv()
                sib_copy(step).start()

    for step in range(1, nh):
        sib_copy(step).wait_recv()
    local[2].wait()

    @pl.loop(0, chunks)
    def _(c):
        for step in range(1, nh):
            at_copy(step, c).wait_recv()

    mt = 256 if mcols % 256 == 0 else 128
    pvel[hx] = jnp.zeros(pvel.shape[1:], pvel.dtype)

    @pl.loop(0, mcols // mt)
    def _(i):
        rows = pl.ds(pl.multiple_of(i * mt, 128), mt)
        mixed = jnp.dot(attn[...], wmine[:, rows], preferred_element_type=jnp.float32)
        hidden = (stream_ref[rows].astype(jnp.float32) + mixed.T).astype(jnp.bfloat16)
        hid_ref[rows] = hidden
        pvel[hx] += jnp.dot(wlat_ref[:, rows], hidden, preferred_element_type=jnp.float32)

    def pv_copy(step):
        return pltpu.make_async_remote_copy(
            src_ref=pvel.at[hx], dst_ref=pvel.at[hx],
            send_sem=pv_send.at[step - 1], recv_sem=pv_recv.at[step - 1],
            device_id={"heads": lax.rem(hx + step, nh)}, device_id_type=MESH)

    for step in range(1, nh):
        pv_copy(step).start()

    @pl.when(jnp.logical_not(has_left))
    def _():
        dext[:, pl.ds(0, 2 * FT)] = jnp.zeros((dext.shape[0], 2 * FT), dext.dtype)

    for step in range(1, nh):
        pv_copy(step).wait_recv()
    velocity = pvel[0]
    for p in range(1, nh):
        velocity = velocity + pvel[p]
    dext[:, pl.ds(2 * FT, tok)] = (lat_ref[...] + step_size * velocity).astype(jnp.bfloat16)
    last = pltpu.make_async_remote_copy(
        src_ref=dext.at[:, pl.ds(tok, 2 * FT)], dst_ref=dext.at[:, pl.ds(0, 2 * FT)],
        send_sem=d_send, recv_sem=d_recv, device_id={"frames": me + 1}, device_id_type=MESH)

    @pl.when(has_right)
    def _():
        last.start()

    @pl.loop(0, chunks)
    def _(c):
        for side in range(2):
            for hop in range(1, hops + 1):
                @pl.when(sends(side, hop))
                def _():
                    for copy in kv_copies(side, hop, c):
                        copy.wait_send()
        for step in range(1, nh):
            at_copy(step, c).wait_send()

    for step in range(1, nh):
        w_copy(step).wait_send()
        sib_copy(step).wait_send()
        pv_copy(step).wait_send()

    @pl.when(has_left)
    def _():
        last.wait_recv()

    den_ref[...] = dext[...]

    @pl.when(has_right)
    def _():
        last.wait_send()


def pack_kernel(n, nh, ng, np_, fh, clip_ref, q_ref, k_ref, v_ref, stream_ref, w_hbm, wlat_ref, lat_ref,
                hid_ref, den_ref,
                bias_ref, stage, msg, tail_stage, tail_msg, res, attn, wmine, pvel, dext,
                m_send, m_recv, t_send, t_recv, at_send, at_recv, w_send, w_recv, g_send, g_recv, s_send, s_recv,
                pv_send, pv_recv, d_send, d_recv, loc):
    me = lax.axis_index("frames")
    hx = lax.axis_index("heads")
    gx = lax.axis_index("groups")
    px = lax.axis_index("pipe")
    tok, feats = q_ref.shape
    heads_here = feats // HD
    model = w_hbm.shape[1]
    mcols = model // nh
    seq_frames = clip_ref.shape[1]
    first = me * fh
    links = (me < n - 1, me > 0)
    arrives = (me > 0, me < n - 1)
    sib = lax.rem(px + 1, np_)

    my_cols = pl.ds(pl.multiple_of(hx * mcols, 128), mcols)
    own_w = pltpu.make_async_copy(
        w_hbm.at[:, my_cols], wmine.at[pl.ds(pl.multiple_of(hx * feats, 128), feats)], loc)
    own_w.start()

    barrier = pltpu.get_barrier_semaphore()
    for side, where in ((0, me + 1), (1, me - 1)):
        @pl.when(links[side])
        def _():
            pl.semaphore_signal(barrier, inc=1, device_id={"frames": where}, device_id_type=MESH)

    for axis, at, size in (("heads", hx, nh), ("groups", gx, ng), ("pipe", px, np_)):
        for step in range(1, size):
            pl.semaphore_signal(barrier, inc=1, device_id={axis: lax.rem(at + step, size)}, device_id_type=MESH)
    pl.semaphore_wait(barrier, links[0].astype(jnp.int32) + links[1].astype(jnp.int32)
                      + (nh - 1) + (ng - 1) + (np_ - 1))

    def clip_at(g):
        return clip_ref[0, jnp.clip(g, 0, seq_frames - 1)]

    def middle(e):
        return (e >= 1) & (e <= n - 2) & (clip_at(fh * e - 1) == clip_at(fh * e + fh))

    am_mid = middle(me)
    to_mid = (middle(me + 1), middle(me - 1))

    def msg_copy(side, c):
        return pltpu.make_async_remote_copy(
            src_ref=stage.at[side, c], dst_ref=msg.at[side, c],
            send_sem=m_send.at[side, c], recv_sem=m_recv.at[side, c],
            device_id={"frames": me + 1 if side == 0 else me - 1}, device_id_type=MESH)

    def tail_copy(side, c):
        return pltpu.make_async_remote_copy(
            src_ref=tail_stage.at[side, c], dst_ref=tail_msg.at[side, c],
            send_sem=t_send.at[side, c], recv_sem=t_recv.at[side, c],
            device_id={"frames": me + 1 if side == 0 else me - 1}, device_id_type=MESH)

    part = feats // (ng * np_)

    def w_rows(origin, group, pipe):
        return pl.ds(pl.multiple_of(origin * feats + (group * np_ + pipe) * part, 64), part)

    def w_copy(step):
        peer = lax.rem(hx + step, nh)
        return pltpu.make_async_remote_copy(
            src_ref=w_hbm.at[pl.ds(pl.multiple_of((gx * np_ + px) * part, 64), part),
                             pl.ds(pl.multiple_of(peer * mcols, 128), mcols)],
            dst_ref=wmine.at[w_rows(hx, gx, px)],
            send_sem=w_send.at[step - 1], recv_sem=w_recv.at[step - 1],
            device_id={"heads": peer}, device_id_type=MESH)

    def g_copy(step, hop):
        rows = w_rows(lax.rem(hx + nh - step, nh), gx, px)
        return pltpu.make_async_remote_copy(
            src_ref=wmine.at[rows], dst_ref=wmine.at[rows],
            send_sem=g_send.at[step - 1, hop - 1], recv_sem=g_recv.at[step - 1, hop - 1],
            device_id={"groups": lax.rem(gx + hop, ng)}, device_id_type=MESH)

    def sib_copy(step, group):
        rows = w_rows(lax.rem(hx + nh - step, nh), group, px)
        return pltpu.make_async_remote_copy(
            src_ref=wmine.at[rows], dst_ref=wmine.at[rows],
            send_sem=s_send.at[step - 1, group], recv_sem=s_recv.at[step - 1, group],
            device_id={"pipe": sib}, device_id_type=MESH)

    def at_copy(step, c):
        cols = pl.ds(pl.multiple_of(hx * feats + c * HD, 128), HD)
        return pltpu.make_async_remote_copy(
            src_ref=attn.at[:, cols], dst_ref=attn.at[:, cols],
            send_sem=at_send.at[step - 1, c], recv_sem=at_recv.at[step - 1, c],
            device_id={"heads": lax.rem(hx + step, nh)}, device_id_type=MESH)

    for step in range(1, nh):
        w_copy(step).start()

    for side in range(2):
        @pl.when(jnp.logical_not(arrives[side]))
        def _():
            msg[side] = jnp.zeros(msg.shape[1:], msg.dtype)
            tail_msg[side] = jnp.zeros(tail_msg.shape[1:], tail_msg.dtype)

    seekers = [j for j in range(fh)] + [-2, -1, fh, fh + 1]
    for i, j in enumerate(seekers):
        mine = clip_at(first + j)
        for e in range(3 * fh):
            g = first + e - fh
            seen = (clip_at(g) == mine) & (g >= 0) & (g < seq_frames)
            bias_ref[pl.ds(i, 1), pl.ds(e * FT, FT)] = jnp.full(
                (1, FT), jnp.where(seen, 0.0, neg_fill), jnp.float32)

    factor = math.log2(math.e) / math.sqrt(HD)
    frame = lambda f: pl.ds(f * FT, FT)

    def send_step(c):
        cols = pl.ds(pl.multiple_of(c * HD, 128), HD)
        ready = am_mid & (c >= LAG)
        old = jnp.maximum(c - LAG, 0)
        for side in range(2):
            spare = 0 if side == 0 else fh - 1
            asks = (fh - 2, fh - 1) if side == 0 else (0, 1)
            for base, ref, ask in ((0, k_ref, asks[0]), (fh, v_ref, asks[1])):
                for f in range(fh):
                    block = ref[frame(f), cols]
                    if f == spare:
                        block = jnp.where(to_mid[side], q_ref[frame(ask), cols], block)
                    if base + f < 2:
                        block = jnp.where(ready, res[1 - side, old, frame(base + f)], block)
                    stage[side, c, frame(base + f)] = block

            @pl.when(links[side])
            def _():
                msg_copy(side, c).start()

    def head_step(c):
        cols = pl.ds(pl.multiple_of(c * HD, 128), HD)
        for i, j in enumerate(seekers):
            if j >= 0 and j < fh:
                asked, lows, highs = q_ref[frame(j), cols], (0, fh), (0, fh)
            else:
                lows, highs = (fh - 2, fh), (0, 2)
                asked = {-2: lambda: msg[0, c, frame(0)], -1: lambda: msg[0, c, frame(fh)],
                         fh: lambda: msg[1, c, frame(fh - 1)], fh + 1: lambda: msg[1, c, frame(2 * fh - 1)]}[j]()
            left = lambda base: msg[0, c, pl.ds((base + lows[0]) * FT, (lows[1] - lows[0]) * FT)]
            right = lambda base: msg[1, c, pl.ds((base + highs[0]) * FT, (highs[1] - highs[0]) * FT)]
            keys = (left(0), k_ref[:, cols], right(0))
            vals = (left(fh), v_ref[:, cols], right(fh))
            spans = (lows, (fh, 2 * fh), (2 * fh + highs[0], 2 * fh + highs[1]))
            scores = []
            for piece, (low, high) in zip(keys, spans):
                dots = lax.dot_general(asked, piece, (((1,), (1,)), ((), ())), preferred_element_type=jnp.float32)
                scores.append(dots + bias_ref[pl.ds(i, 1), pl.ds(low * FT, (high - low) * FT)])
            top = functools.reduce(jnp.maximum, [jnp.max(x, axis=1, keepdims=True) for x in scores])
            expo = [jnp.exp2((x - top) * factor) for x in scores]
            total = sum(jnp.sum(x, axis=1, keepdims=True) for x in expo)
            summed = sum(jnp.dot(x.astype(jnp.bfloat16), y, preferred_element_type=jnp.float32)
                         for x, y in zip(expo, vals))
            out = (summed / total).astype(jnp.bfloat16)
            if j >= 0 and j < fh:
                attn[frame(j), pl.ds(pl.multiple_of(hx * feats + c * HD, 128), HD)] = out
            elif j < 0:
                res[0, c, frame(j + 2)] = out
            else:
                res[1, c, frame(j - fh)] = out

    def settle(c, come):
        cols = pl.ds(pl.multiple_of(hx * feats + c * HD, 128), HD)
        for j in range(fh):
            block = attn[frame(j), cols]
            here = clip_at(first + j)
            if j < 2:
                block = jnp.where(to_mid[1] & (here == clip_at(first - 1)), come(0, j), block)
            if j >= fh - 2:
                block = jnp.where(to_mid[0] & (here == clip_at(first + fh)), come(1, j - (fh - 2)), block)
            attn[frame(j), cols] = block
        for step in range(1, nh):
            at_copy(step, c).start()

    @pl.loop(0, heads_here + LAG + AHEAD)
    def _(t):
        @pl.when(t < heads_here)
        def _():
            send_step(t)

        @pl.when((t >= heads_here) & (t < heads_here + LAG))
        def _():
            for side in range(2):
                tail_stage[side, t - heads_here] = res[1 - side, t - LAG]

                @pl.when(links[side])
                def _():
                    tail_copy(side, t - heads_here).start()

        m = t - AHEAD

        @pl.when((m >= 0) & (m < heads_here))
        def _():
            for side in range(2):
                @pl.when(arrives[side])
                def _():
                    msg_copy(side, m).wait_recv()
            head_step(m)

        @pl.when((m >= LAG) & (m < heads_here))
        def _():
            settle(m - LAG, lambda side, row: msg[side, m, frame(row)])

        @pl.when(m >= heads_here)
        def _():
            for side in range(2):
                @pl.when(arrives[side])
                def _():
                    tail_copy(side, m - heads_here).wait_recv()
            settle(m - LAG, lambda side, row: tail_msg[side, m - heads_here, frame(row)])

        @pl.when(t == heads_here // 2 + 1)
        def _():
            for step in range(1, nh):
                w_copy(step).wait_recv()
                for hop in range(1, ng):
                    g_copy(step, hop).start()
                sib_copy(step, gx).start()

        @pl.when(t == heads_here + LAG - 1)
        def _():
            for step in range(1, nh):
                for hop in range(1, ng):
                    g_copy(step, hop).wait_recv()
                for hop in range(1, ng):
                    sib_copy(step, lax.rem(gx + hop, ng)).start()

    for step in range(1, nh):
        for group in range(ng):
            sib_copy(step, group).wait_recv()
    own_w.wait()

    @pl.loop(0, heads_here)
    def _(c):
        for step in range(1, nh):
            at_copy(step, c).wait_recv()

    mt = 256 if mcols % 256 == 0 else 128
    pvel[hx] = jnp.zeros(pvel.shape[1:], pvel.dtype)

    @pl.loop(0, mcols // mt)
    def _(i):
        rows = pl.ds(pl.multiple_of(i * mt, 128), mt)
        mixed = jnp.dot(attn[...], wmine[:, rows], preferred_element_type=jnp.float32)
        hidden = (stream_ref[rows].astype(jnp.float32) + mixed.T).astype(jnp.bfloat16)
        hid_ref[rows] = hidden
        pvel[hx] += jnp.dot(wlat_ref[:, rows], hidden, preferred_element_type=jnp.float32)

    def pv_copy(step):
        return pltpu.make_async_remote_copy(
            src_ref=pvel.at[hx], dst_ref=pvel.at[hx],
            send_sem=pv_send.at[step - 1], recv_sem=pv_recv.at[step - 1],
            device_id={"heads": lax.rem(hx + step, nh)}, device_id_type=MESH)

    for step in range(1, nh):
        pv_copy(step).start()

    @pl.when(jnp.logical_not(links[1]))
    def _():
        dext[:, pl.ds(0, 2 * FT)] = jnp.zeros((dext.shape[0], 2 * FT), dext.dtype)

    @pl.loop(0, heads_here)
    def _(c):
        for side in range(2):
            @pl.when(links[side])
            def _():
                msg_copy(side, c).wait_send()
        for step in range(1, nh):
            at_copy(step, c).wait_send()

    for c in range(LAG):
        for side in range(2):
            @pl.when(links[side])
            def _():
                tail_copy(side, c).wait_send()

    for step in range(1, nh):
        w_copy(step).wait_send()
        for hop in range(1, ng):
            g_copy(step, hop).wait_send()
        for group in range(ng):
            sib_copy(step, group).wait_send()

    for step in range(1, nh):
        pv_copy(step).wait_recv()
    velocity = pvel[0]
    for p in range(1, nh):
        velocity = velocity + pvel[p]
    dext[:, pl.ds(2 * FT, tok)] = (lat_ref[...] + step_size * velocity).astype(jnp.bfloat16)
    last = pltpu.make_async_remote_copy(
        src_ref=dext.at[:, pl.ds(tok, 2 * FT)], dst_ref=dext.at[:, pl.ds(0, 2 * FT)],
        send_sem=d_send, recv_sem=d_recv, device_id={"frames": me + 1}, device_id_type=MESH)

    @pl.when(links[0])
    def _():
        last.start()

    for step in range(1, nh):
        pv_copy(step).wait_send()

    @pl.when(links[1])
    def _():
        last.wait_recv()

    den_ref[...] = dext[...]

    @pl.when(links[0])
    def _():
        last.wait_send()


def conv_kernel(fh, clip_ref, den_ref, w_ref, bias_ref, hid_ref, out_ref, hid_out, patch, held, sem):
    load_hidden = pltpu.make_async_copy(hid_ref, held, sem.at[0])
    load_hidden.start()
    save_hidden = pltpu.make_async_copy(held, hid_out, sem.at[1])
    first = lax.axis_index("frames") * fh
    pix = 4 * FT
    row64 = lax.broadcasted_iota(jnp.int32, (LAT_CH, 4 * LAT_CH), 1)
    ch = lax.broadcasted_iota(jnp.int32, (LAT_CH, 4 * LAT_CH), 0)
    tokn = lax.broadcasted_iota(jnp.int32, (FT, pix), 0)
    where = lax.broadcasted_iota(jnp.int32, (FT, pix), 1)
    lane = lax.broadcasted_iota(jnp.int32, (LAT_CH, pix), 1)
    width = 2 * FW
    ypos, xpos = lane // width, lane % width
    selects, places = [], []
    for phase in range(4):
        p, q = phase // 2, phase % 2
        selects.append((row64 == 4 * ch + phase).astype(jnp.bfloat16))
        target = (2 * (tokn // FW) + p) * width + 2 * (tokn % FW) + q
        places.append((where == target).astype(jnp.bfloat16))
    for e in range(fh + 2):
        frame = den_ref[:, pl.ds(e * FT, FT)]
        image = jnp.zeros((LAT_CH, pix), jnp.float32)
        for phase in range(4):
            rows = jnp.dot(selects[phase], frame, preferred_element_type=jnp.float32).astype(jnp.bfloat16)
            image = image + jnp.dot(rows, places[phase], preferred_element_type=jnp.float32)
        for i in range(3):
            for j in range(3):
                shift = (i - 1) * width + (j - 1)
                moved = pltpu.roll(image, (-shift) % pix, 1) if shift else image
                ok = ((ypos + (i - 1) >= 0) & (ypos + (i - 1) < 2 * FH)
                      & (xpos + (j - 1) >= 0) & (xpos + (j - 1) < width))
                patch[e, pl.ds((3 * i + j) * LAT_CH, LAT_CH)] = jnp.where(ok, moved, 0.0).astype(jnp.bfloat16)
    load_hidden.wait()
    save_hidden.start()
    bias = bias_ref[...].T
    for f in range(fh):
        here = clip_ref[0, first + f]
        back1 = jnp.where((first + f >= 1) & (clip_ref[0, jnp.maximum(first + f - 1, 0)] == here), 1, 0)
        back2 = jnp.where((first + f >= 2) & (clip_ref[0, jnp.maximum(first + f - 2, 0)] == here), 2, back1)
        rows = jnp.concatenate([patch[f + 2 - back2], patch[f + 2 - back1], patch[f + 2]], axis=0)
        conv = lax.dot_general(w_ref[...], rows, (((0,), (0,)), ((), ())), preferred_element_type=jnp.float32)
        out_ref[f] = (conv + bias).astype(jnp.bfloat16)
    save_hidden.wait()


def shards(n, nh, ng, np_, query, key, value, stream, w_out, w_lat, latent, frame_clip, w_conv, conv_bias):
    tok, feats = query.shape[1:]
    fh = tok // FT
    seq_frames = frame_clip.shape[1]
    halo = seq_frames // 2 - 1
    hops = -(-halo // fh)
    chunks = feats // HD // CHUNK
    model, mcols = w_out.shape[1], stream.shape[1]
    latp = w_lat.shape[1]
    ext = (2 * halo + fh) * FT
    vmem = pl.BlockSpec(memory_space=pltpu.VMEM)
    hbm = pl.BlockSpec(memory_space=pl.ANY)
    smem = pl.BlockSpec(memory_space=pltpu.SMEM)
    peers = max(1, nh - 1)
    dma = pltpu.SemaphoreType.DMA
    heads_here = feats // HD
    results = (jax.ShapeDtypeStruct((mcols, tok), jnp.bfloat16),
               jax.ShapeDtypeStruct((latp, tok + 2 * FT), jnp.bfloat16))
    params = pltpu.CompilerParams(collective_id=0, has_side_effects=True, vmem_limit_bytes=56 * 1024 * 1024)
    operands = (frame_clip, query[0], key[0], value[0], stream[0], w_out, w_lat.T, latent[0])
    pack = pl.pallas_call(
        functools.partial(pack_kernel, n, nh, ng, np_, fh),
        out_shape=results,
        in_specs=[smem, vmem, vmem, vmem, vmem, hbm, vmem, vmem],
        out_specs=(vmem, vmem),
        scratch_shapes=[
            pltpu.VMEM((fh + 4, 3 * fh * FT), jnp.float32),
            pltpu.VMEM((2, heads_here, 2 * fh * FT, HD), jnp.bfloat16),
            pltpu.VMEM((2, heads_here, 2 * fh * FT, HD), jnp.bfloat16),
            pltpu.VMEM((2, LAG, 2 * FT, HD), jnp.bfloat16),
            pltpu.VMEM((2, LAG, 2 * FT, HD), jnp.bfloat16),
            pltpu.VMEM((2, heads_here, 2 * FT, HD), jnp.bfloat16),
            pltpu.VMEM((tok, nh * feats), jnp.bfloat16),
            pltpu.VMEM((nh * feats, mcols), jnp.bfloat16),
            pltpu.VMEM((nh, latp, tok), jnp.float32),
            pltpu.VMEM((latp, tok + 2 * FT), jnp.bfloat16),
            dma((2, heads_here)), dma((2, heads_here)),
            dma((2, LAG)), dma((2, LAG)),
            dma((peers, heads_here)), dma((peers, heads_here)),
            dma((peers,)), dma((peers,)),
            dma((peers, ng)), dma((peers, ng)),
            dma((peers, ng)), dma((peers, ng)),
            dma((peers,)), dma((peers,)),
            dma(()), dma(()), dma(()),
        ],
        compiler_params=params,
        name="clip_pack",
    )
    chain = pl.pallas_call(
        functools.partial(block_kernel, n, nh, np_, halo, fh),
        out_shape=results,
        in_specs=[smem, vmem, hbm, hbm, vmem, hbm, vmem, vmem],
        out_specs=(vmem, vmem),
        scratch_shapes=[
            pltpu.VMEM((fh, (2 * halo + 1) * FT), jnp.float32),
            pltpu.VMEM((ext, feats), jnp.bfloat16),
            pltpu.VMEM((ext, feats), jnp.bfloat16),
            pltpu.VMEM((tok, nh * feats), jnp.bfloat16),
            pltpu.VMEM((nh * feats, mcols), jnp.bfloat16),
            pltpu.VMEM((nh, latp, tok), jnp.float32),
            pltpu.VMEM((latp, tok + 2 * FT), jnp.bfloat16),
            dma((2, hops, chunks, 2)), dma((2, hops, chunks, 2)),
            dma((peers, chunks)), dma((peers, chunks)),
            dma((peers,)), dma((peers,)),
            dma((peers,)), dma((peers,)),
            dma((peers,)), dma((peers,)),
            dma(()), dma(()), dma((3,)),
        ],
        compiler_params=params,
        name="clip_block",
    )
    fits = fh == 3 and seq_frames // 2 <= 2 * fh
    hidden, den = (pack if fits else chain)(*operands)

    outs = w_conv.shape[0]
    feat, hidden = pl.pallas_call(
        functools.partial(conv_kernel, fh),
        out_shape=(jax.ShapeDtypeStruct((fh, outs, 4 * FT), jnp.bfloat16),
                   jax.ShapeDtypeStruct((mcols, tok), jnp.bfloat16)),
        in_specs=[smem, vmem, vmem, vmem, hbm],
        out_specs=(vmem, hbm),
        scratch_shapes=[pltpu.VMEM((fh + 2, 9 * LAT_CH, 4 * FT), jnp.bfloat16),
                        pltpu.VMEM((mcols, tok), jnp.bfloat16), dma((2,))],
        name="causal_conv",
    )(frame_clip, den, w_conv.T, conv_bias[None, :], hidden)
    return (hidden[None], jnp.transpose(feat, (1, 0, 2))[None])


def solution(mesh):
    sizes = dict(mesh.shape)
    return jax.shard_map(
        functools.partial(shards, sizes["frames"], sizes["heads"], sizes["groups"], sizes["pipe"]),
        mesh=mesh,
        in_specs=(
            P(("groups", "pipe"), "frames", "heads"),
            P(("groups", "pipe"), "frames", "heads"),
            P(("groups", "pipe"), "frames", "heads"),
            P(("groups", "pipe"), "heads", "frames"),
            P("heads", None),
            P("heads", None),
            P(("groups", "pipe"), None, "frames"),
            P(("groups", "pipe"), None),
            P("heads", None),
            P("heads"),
        ),
        out_specs=(
            P(("groups", "pipe"), "heads", "frames"),
            P(("groups", "pipe"), "heads", "frames", None),
        ),
        check_vma=False,
    )
```

```python
import functools
import math

import jax
import jax.numpy as jnp
from jax import lax
from jax.experimental import pallas as pl
from jax.experimental.pallas import tpu as pltpu
from jax.sharding import PartitionSpec as P

HD = 128
LAT_CH = 16
FH = 8
FW = 16
FT = FH * FW
CHUNK = 1
AHEAD = 2
LAG = AHEAD + 1
PIECES = 2
MESH = pl.DeviceIdType.MESH

neg_fill = -1e30
step_size = -0.5


def block_kernel(n, nh, np_, halo, fh, clip_ref, q_ref, k_hbm, v_hbm, stream_ref, w_hbm, wlat_ref, lat_ref,
                 hid_ref, den_ref,
                 bias_ref, kext, vext, attn, wmine, pvel, dext,
                 kv_send, kv_recv, at_send, at_recv, w_send, w_recv, s_send, s_recv, pv_send, pv_recv,
                 d_send, d_recv, loc):
    me = lax.axis_index("frames")
    hx = lax.axis_index("heads")
    px = lax.axis_index("pipe")
    tok, feats = q_ref.shape
    heads_here = feats // HD
    chunks = heads_here // CHUNK
    cw = CHUNK * HD
    hops = -(-halo // fh)
    model = w_hbm.shape[1]
    mcols = model // nh
    own0 = halo * FT
    has_right = me < n - 1
    has_left = me > 0
    sib = lax.rem(px + 1, np_)

    my_cols = pl.ds(pl.multiple_of(hx * mcols, 128), mcols)
    my_rows = pl.ds(pl.multiple_of(hx * feats, 128), feats)
    local = [
        pltpu.make_async_copy(k_hbm, kext.at[pl.ds(own0, tok)], loc.at[0]),
        pltpu.make_async_copy(v_hbm, vext.at[pl.ds(own0, tok)], loc.at[1]),
        pltpu.make_async_copy(w_hbm.at[:, my_cols], wmine.at[my_rows], loc.at[2]),
    ]
    for copy in local:
        copy.start()

    barrier = pltpu.get_barrier_semaphore()

    @pl.when(has_left)
    def _():
        pl.semaphore_signal(barrier, inc=1, device_id={"frames": me - 1}, device_id_type=MESH)

    @pl.when(has_right)
    def _():
        pl.semaphore_signal(barrier, inc=1, device_id={"frames": me + 1}, device_id_type=MESH)

    for step in range(1, nh):
        pl.semaphore_signal(barrier, inc=1, device_id={"heads": lax.rem(hx + step, nh)}, device_id_type=MESH)
    pl.semaphore_signal(barrier, inc=1, device_id={"pipe": sib}, device_id_type=MESH)
    pl.semaphore_wait(barrier, has_left.astype(jnp.int32) + has_right.astype(jnp.int32) + (nh - 1) + 1)

    def span(side, hop):
        if side == 0:
            low, high = max(0, halo - fh * hop), halo - fh * (hop - 1)
        else:
            low, high = halo + fh * hop, min(2 * halo + fh, halo + fh * (hop + 1))
        return low * FT, (high - low) * FT

    def kv_copies(side, hop, c):
        low, size = span(side, hop)
        cols = pl.ds(pl.multiple_of(c * cw, 128), cw)
        shift = fh * FT if side == 0 else -fh * FT
        made = []
        for which, (hbm, ext) in enumerate(((k_hbm, kext), (v_hbm, vext))):
            if hop == 1:
                src = hbm.at[pl.ds(low + shift - own0, size), cols]
            else:
                src = ext.at[pl.ds(low + shift, size), cols]
            made.append(pltpu.make_async_remote_copy(
                src_ref=src,
                dst_ref=ext.at[pl.ds(low, size), cols],
                send_sem=kv_send.at[side, hop - 1, c, which],
                recv_sem=kv_recv.at[side, hop - 1, c, which],
                device_id={"frames": me + 1 if side == 0 else me - 1},
                device_id_type=MESH,
            ))
        return made

    def sends(side, hop):
        if side == 0:
            return has_right & (me - (hop - 1) >= 0)
        return has_left & (me + (hop - 1) <= n - 1)

    def receives(side, hop):
        return me - hop >= 0 if side == 0 else me + hop <= n - 1

    def start_hop(hop, c):
        for side in range(2):
            @pl.when(sends(side, hop))
            def _():
                for copy in kv_copies(side, hop, c):
                    copy.start()

    def await_hop(hop, c):
        for side in range(2):
            @pl.when(receives(side, hop))
            def _():
                for copy in kv_copies(side, hop, c):
                    copy.wait_recv()

    half = feats // np_

    def w_copy(step):
        peer = lax.rem(hx + step, nh)
        return pltpu.make_async_remote_copy(
            src_ref=w_hbm.at[pl.ds(pl.multiple_of(px * half, 128), half),
                             pl.ds(pl.multiple_of(peer * mcols, 128), mcols)],
            dst_ref=wmine.at[pl.ds(pl.multiple_of(hx * feats + px * half, 128), half)],
            send_sem=w_send.at[step - 1], recv_sem=w_recv.at[step - 1],
            device_id={"heads": peer}, device_id_type=MESH)

    def sib_copy(step):
        origin = lax.rem(hx + nh - step, nh)
        rows = pl.ds(pl.multiple_of(origin * feats + px * half, 128), half)
        return pltpu.make_async_remote_copy(
            src_ref=wmine.at[rows], dst_ref=wmine.at[rows],
            send_sem=s_send.at[step - 1], recv_sem=s_recv.at[step - 1],
            device_id={"pipe": sib}, device_id_type=MESH)

    def at_copy(step, c):
        cols = pl.ds(pl.multiple_of(hx * feats + c * cw, 128), cw)
        return pltpu.make_async_remote_copy(
            src_ref=attn.at[:, cols], dst_ref=attn.at[:, cols],
            send_sem=at_send.at[step - 1, c], recv_sem=at_recv.at[step - 1, c],
            device_id={"heads": lax.rem(hx + step, nh)}, device_id_type=MESH)

    start_hop(1, 0)
    for step in range(1, nh):
        w_copy(step).start()

    for side in range(2):
        for hop in range(1, hops + 1):
            low, size = span(side, hop)

            @pl.when(jnp.logical_not(receives(side, hop)))
            def _():
                kext[pl.ds(low, size)] = jnp.zeros((size, feats), kext.dtype)
                vext[pl.ds(low, size)] = jnp.zeros((size, feats), vext.dtype)

    seq_frames = clip_ref.shape[1]
    first = me * fh
    for j in range(fh):
        for e in range(2 * halo + 1):
            g = first + j + e - halo
            seen = clip_ref[0, jnp.clip(g, 0, seq_frames - 1)] == clip_ref[0, first + j]
            seen = seen & (g >= 0) & (g < seq_frames)
            bias_ref[pl.ds(j, 1), pl.ds(e * FT, FT)] = jnp.full(
                (1, FT), jnp.where(seen, 0.0, neg_fill), jnp.float32)

    local[0].wait()
    local[1].wait()

    band = (2 * halo + 1) * FT
    factor = math.log2(math.e) / math.sqrt(HD)

    def head_step(c, inner):
        col = pl.multiple_of(c * cw + inner * HD, 128)
        cols = pl.ds(col, HD)
        for j in range(fh):
            rows = pl.ds(j * FT, FT)
            scores = lax.dot_general(
                q_ref[rows, cols], kext[pl.ds(j * FT, band), cols], (((1,), (1,)), ((), ())),
                preferred_element_type=jnp.float32)
            scores = scores + bias_ref[pl.ds(j, 1)]
            top = jnp.max(scores, axis=1, keepdims=True)
            expo = jnp.exp2((scores - top) * factor)
            total = jnp.sum(expo, axis=1, keepdims=True)
            summed = jnp.dot(expo.astype(jnp.bfloat16), vext[pl.ds(j * FT, band), cols],
                             preferred_element_type=jnp.float32)
            attn[rows, pl.ds(pl.multiple_of(hx * feats + col, 128), HD)] = (summed / total).astype(jnp.bfloat16)

    @pl.loop(0, chunks + hops)
    def _(t):
        @pl.when(t + 1 < chunks)
        def _():
            start_hop(1, t + 1)

        for hop in range(2, hops + 1):
            c = t - (hop - 2)

            @pl.when((c >= 0) & (c < chunks))
            def _():
                await_hop(hop - 1, c)
                start_hop(hop, c)

        done = t - hops

        @pl.when(done >= 0)
        def _():
            await_hop(hops, done)

            @pl.loop(0, CHUNK)
            def _(inner):
                head_step(done, inner)

            for step in range(1, nh):
                at_copy(step, done).start()

        @pl.when(t == chunks + hops - 2)
        def _():
            for step in range(1, nh):
                w_copy(step).wait_recv()
                sib_copy(step).start()

    for step in range(1, nh):
        sib_copy(step).wait_recv()
    local[2].wait()

    @pl.loop(0, chunks)
    def _(c):
        for step in range(1, nh):
            at_copy(step, c).wait_recv()

    mt = 256 if mcols % 256 == 0 else 128
    pvel[hx] = jnp.zeros(pvel.shape[1:], pvel.dtype)

    @pl.loop(0, mcols // mt)
    def _(i):
        rows = pl.ds(pl.multiple_of(i * mt, 128), mt)
        mixed = jnp.dot(attn[...], wmine[:, rows], preferred_element_type=jnp.float32)
        hidden = (stream_ref[rows].astype(jnp.float32) + mixed.T).astype(jnp.bfloat16)
        hid_ref[rows] = hidden
        pvel[hx] += jnp.dot(wlat_ref[:, rows], hidden, preferred_element_type=jnp.float32)

    def pv_copy(step):
        return pltpu.make_async_remote_copy(
            src_ref=pvel.at[hx], dst_ref=pvel.at[hx],
            send_sem=pv_send.at[step - 1], recv_sem=pv_recv.at[step - 1],
            device_id={"heads": lax.rem(hx + step, nh)}, device_id_type=MESH)

    for step in range(1, nh):
        pv_copy(step).start()

    @pl.when(jnp.logical_not(has_left))
    def _():
        dext[:, pl.ds(0, 2 * FT)] = jnp.zeros((dext.shape[0], 2 * FT), dext.dtype)

    for step in range(1, nh):
        pv_copy(step).wait_recv()
    velocity = pvel[0]
    for p in range(1, nh):
        velocity = velocity + pvel[p]
    dext[:, pl.ds(2 * FT, tok)] = (lat_ref[...] + step_size * velocity).astype(jnp.bfloat16)
    last = pltpu.make_async_remote_copy(
        src_ref=dext.at[:, pl.ds(tok, 2 * FT)], dst_ref=dext.at[:, pl.ds(0, 2 * FT)],
        send_sem=d_send, recv_sem=d_recv, device_id={"frames": me + 1}, device_id_type=MESH)

    @pl.when(has_right)
    def _():
        last.start()

    @pl.loop(0, chunks)
    def _(c):
        for side in range(2):
            for hop in range(1, hops + 1):
                @pl.when(sends(side, hop))
                def _():
                    for copy in kv_copies(side, hop, c):
                        copy.wait_send()
        for step in range(1, nh):
            at_copy(step, c).wait_send()

    for step in range(1, nh):
        w_copy(step).wait_send()
        sib_copy(step).wait_send()
        pv_copy(step).wait_send()

    @pl.when(has_left)
    def _():
        last.wait_recv()

    den_ref[...] = dext[...]

    @pl.when(has_right)
    def _():
        last.wait_send()


def pack_kernel(n, nh, ng, np_, fh, clip_ref, q_ref, k_ref, v_ref, stream_ref, w_hbm, wlat_ref, lat_ref,
                hid_ref, den_ref,
                bias_ref, stage, msg, tail_stage, tail_msg, res, attn, wmine, pvel, dext,
                m_send, m_recv, t_send, t_recv, at_send, at_recv, w_send, w_recv, g_send, g_recv, s_send, s_recv,
                pv_send, pv_recv, d_send, d_recv, loc):
    me = lax.axis_index("frames")
    hx = lax.axis_index("heads")
    gx = lax.axis_index("groups")
    px = lax.axis_index("pipe")
    tok, feats = q_ref.shape
    heads_here = feats // HD
    model = w_hbm.shape[1]
    mcols = model // nh
    seq_frames = clip_ref.shape[1]
    first = me * fh
    links = (me < n - 1, me > 0)
    arrives = (me > 0, me < n - 1)
    sib = lax.rem(px + 1, np_)

    my_cols = pl.ds(pl.multiple_of(hx * mcols, 128), mcols)
    own_w = pltpu.make_async_copy(
        w_hbm.at[:, my_cols], wmine.at[pl.ds(pl.multiple_of(hx * feats, 128), feats)], loc)
    own_w.start()

    barrier = pltpu.get_barrier_semaphore()
    for side, where in ((0, me + 1), (1, me - 1)):
        @pl.when(links[side])
        def _():
            pl.semaphore_signal(barrier, inc=1, device_id={"frames": where}, device_id_type=MESH)

    for axis, at, size in (("heads", hx, nh), ("groups", gx, ng), ("pipe", px, np_)):
        for step in range(1, size):
            pl.semaphore_signal(barrier, inc=1, device_id={axis: lax.rem(at + step, size)}, device_id_type=MESH)
    pl.semaphore_wait(barrier, links[0].astype(jnp.int32) + links[1].astype(jnp.int32)
                      + (nh - 1) + (ng - 1) + (np_ - 1))

    def clip_at(g):
        return clip_ref[0, jnp.clip(g, 0, seq_frames - 1)]

    def middle(e):
        return (e >= 1) & (e <= n - 2) & (clip_at(fh * e - 1) == clip_at(fh * e + fh))

    am_mid = middle(me)
    to_mid = (middle(me + 1), middle(me - 1))

    def msg_copy(side, c):
        return pltpu.make_async_remote_copy(
            src_ref=stage.at[side, c], dst_ref=msg.at[side, c],
            send_sem=m_send.at[side, c], recv_sem=m_recv.at[side, c],
            device_id={"frames": me + 1 if side == 0 else me - 1}, device_id_type=MESH)

    def tail_copy(side, c):
        return pltpu.make_async_remote_copy(
            src_ref=tail_stage.at[side, c], dst_ref=tail_msg.at[side, c],
            send_sem=t_send.at[side, c], recv_sem=t_recv.at[side, c],
            device_id={"frames": me + 1 if side == 0 else me - 1}, device_id_type=MESH)

    part = feats // (ng * np_ * PIECES)

    def w_rows(origin, group, pipe, piece):
        return pl.ds(pl.multiple_of(origin * feats + ((group * np_ + pipe) * PIECES + piece) * part, 64), part)

    def w_copy(step, piece):
        peer = lax.rem(hx + step, nh)
        return pltpu.make_async_remote_copy(
            src_ref=w_hbm.at[pl.ds(pl.multiple_of(((gx * np_ + px) * PIECES + piece) * part, 64), part),
                             pl.ds(pl.multiple_of(peer * mcols, 128), mcols)],
            dst_ref=wmine.at[w_rows(hx, gx, px, piece)],
            send_sem=w_send.at[step - 1, piece], recv_sem=w_recv.at[step - 1, piece],
            device_id={"heads": peer}, device_id_type=MESH)

    def g_copy(step, hop, piece):
        rows = w_rows(lax.rem(hx + nh - step, nh), gx, px, piece)
        return pltpu.make_async_remote_copy(
            src_ref=wmine.at[rows], dst_ref=wmine.at[rows],
            send_sem=g_send.at[step - 1, hop - 1, piece], recv_sem=g_recv.at[step - 1, hop - 1, piece],
            device_id={"groups": lax.rem(gx + hop, ng)}, device_id_type=MESH)

    def sib_copy(step, group, piece):
        rows = w_rows(lax.rem(hx + nh - step, nh), group, px, piece)
        return pltpu.make_async_remote_copy(
            src_ref=wmine.at[rows], dst_ref=wmine.at[rows],
            send_sem=s_send.at[step - 1, group, piece], recv_sem=s_recv.at[step - 1, group, piece],
            device_id={"pipe": sib}, device_id_type=MESH)

    def at_copy(step, c):
        cols = pl.ds(pl.multiple_of(hx * feats + c * HD, 128), HD)
        return pltpu.make_async_remote_copy(
            src_ref=attn.at[:, cols], dst_ref=attn.at[:, cols],
            send_sem=at_send.at[step - 1, c], recv_sem=at_recv.at[step - 1, c],
            device_id={"heads": lax.rem(hx + step, nh)}, device_id_type=MESH)

    for step in range(1, nh):
        for piece in range(PIECES):
            w_copy(step, piece).start()

    for side in range(2):
        @pl.when(jnp.logical_not(arrives[side]))
        def _():
            msg[side] = jnp.zeros(msg.shape[1:], msg.dtype)
            tail_msg[side] = jnp.zeros(tail_msg.shape[1:], tail_msg.dtype)

    seekers = [j for j in range(fh)] + [-2, -1, fh, fh + 1]
    for i, j in enumerate(seekers):
        mine = clip_at(first + j)
        for e in range(3 * fh):
            g = first + e - fh
            seen = (clip_at(g) == mine) & (g >= 0) & (g < seq_frames)
            bias_ref[pl.ds(i, 1), pl.ds(e * FT, FT)] = jnp.full(
                (1, FT), jnp.where(seen, 0.0, neg_fill), jnp.float32)

    factor = math.log2(math.e) / math.sqrt(HD)
    frame = lambda f: pl.ds(f * FT, FT)

    def send_step(c):
        cols = pl.ds(pl.multiple_of(c * HD, 128), HD)
        ready = am_mid & (c >= LAG)
        old = jnp.maximum(c - LAG, 0)
        for side in range(2):
            spare = 0 if side == 0 else fh - 1
            asks = (fh - 2, fh - 1) if side == 0 else (0, 1)
            for base, ref, ask in ((0, k_ref, asks[0]), (fh, v_ref, asks[1])):
                for f in range(fh):
                    block = ref[frame(f), cols]
                    if f == spare:
                        block = jnp.where(to_mid[side], q_ref[frame(ask), cols], block)
                    if base + f < 2:
                        block = jnp.where(ready, res[1 - side, old, frame(base + f)], block)
                    stage[side, c, frame(base + f)] = block

            @pl.when(links[side])
            def _():
                msg_copy(side, c).start()

    def head_step(c):
        cols = pl.ds(pl.multiple_of(c * HD, 128), HD)
        for i, j in enumerate(seekers):
            if j >= 0 and j < fh:
                asked, lows, highs = q_ref[frame(j), cols], (0, fh), (0, fh)
            else:
                lows, highs = (fh - 2, fh), (0, 2)
                asked = {-2: lambda: msg[0, c, frame(0)], -1: lambda: msg[0, c, frame(fh)],
                         fh: lambda: msg[1, c, frame(fh - 1)], fh + 1: lambda: msg[1, c, frame(2 * fh - 1)]}[j]()
            left = lambda base: msg[0, c, pl.ds((base + lows[0]) * FT, (lows[1] - lows[0]) * FT)]
            right = lambda base: msg[1, c, pl.ds((base + highs[0]) * FT, (highs[1] - highs[0]) * FT)]
            keys = (left(0), k_ref[:, cols], right(0))
            vals = (left(fh), v_ref[:, cols], right(fh))
            spans = (lows, (fh, 2 * fh), (2 * fh + highs[0], 2 * fh + highs[1]))
            scores = []
            for piece, (low, high) in zip(keys, spans):
                dots = lax.dot_general(asked, piece, (((1,), (1,)), ((), ())), preferred_element_type=jnp.float32)
                scores.append(dots + bias_ref[pl.ds(i, 1), pl.ds(low * FT, (high - low) * FT)])
            top = functools.reduce(jnp.maximum, [jnp.max(x, axis=1, keepdims=True) for x in scores])
            expo = [jnp.exp2((x - top) * factor) for x in scores]
            total = sum(jnp.sum(x, axis=1, keepdims=True) for x in expo)
            summed = sum(jnp.dot(x.astype(jnp.bfloat16), y, preferred_element_type=jnp.float32)
                         for x, y in zip(expo, vals))
            out = (summed / total).astype(jnp.bfloat16)
            if j >= 0 and j < fh:
                attn[frame(j), pl.ds(pl.multiple_of(hx * feats + c * HD, 128), HD)] = out
            elif j < 0:
                res[0, c, frame(j + 2)] = out
            else:
                res[1, c, frame(j - fh)] = out

    def settle(c, come):
        cols = pl.ds(pl.multiple_of(hx * feats + c * HD, 128), HD)
        for j in range(fh):
            block = attn[frame(j), cols]
            here = clip_at(first + j)
            if j < 2:
                block = jnp.where(to_mid[1] & (here == clip_at(first - 1)), come(0, j), block)
            if j >= fh - 2:
                block = jnp.where(to_mid[0] & (here == clip_at(first + fh)), come(1, j - (fh - 2)), block)
            attn[frame(j), cols] = block
        for step in range(1, nh):
            at_copy(step, c).start()

    @pl.loop(0, heads_here + LAG + AHEAD)
    def _(t):
        @pl.when(t < heads_here)
        def _():
            send_step(t)

        @pl.when((t >= heads_here) & (t < heads_here + LAG))
        def _():
            for side in range(2):
                tail_stage[side, t - heads_here] = res[1 - side, t - LAG]

                @pl.when(links[side])
                def _():
                    tail_copy(side, t - heads_here).start()

        m = t - AHEAD

        @pl.when((m >= 0) & (m < heads_here))
        def _():
            for side in range(2):
                @pl.when(arrives[side])
                def _():
                    msg_copy(side, m).wait_recv()
            head_step(m)

        @pl.when((m >= LAG) & (m < heads_here))
        def _():
            settle(m - LAG, lambda side, row: msg[side, m, frame(row)])

        @pl.when(m >= heads_here)
        def _():
            for side in range(2):
                @pl.when(arrives[side])
                def _():
                    tail_copy(side, m - heads_here).wait_recv()
            settle(m - LAG, lambda side, row: tail_msg[side, m - heads_here, frame(row)])

        for piece in range(PIECES):
            @pl.when(t == (heads_here // 4) * (piece + 1))
            def _():
                for step in range(1, nh):
                    w_copy(step, piece).wait_recv()
                    for hop in range(1, ng):
                        g_copy(step, hop, piece).start()
                    sib_copy(step, gx, piece).start()

            @pl.when(t == (heads_here // 4) * (piece + 1) + heads_here // 2)
            def _():
                for step in range(1, nh):
                    for hop in range(1, ng):
                        g_copy(step, hop, piece).wait_recv()
                    for hop in range(1, ng):
                        sib_copy(step, lax.rem(gx + hop, ng), piece).start()

    for step in range(1, nh):
        for group in range(ng):
            for piece in range(PIECES):
                sib_copy(step, group, piece).wait_recv()
    own_w.wait()

    @pl.loop(0, heads_here)
    def _(c):
        for step in range(1, nh):
            at_copy(step, c).wait_recv()

    mt = 256 if mcols % 256 == 0 else 128
    pvel[hx] = jnp.zeros(pvel.shape[1:], pvel.dtype)

    @pl.loop(0, mcols // mt)
    def _(i):
        rows = pl.ds(pl.multiple_of(i * mt, 128), mt)
        mixed = jnp.dot(attn[...], wmine[:, rows], preferred_element_type=jnp.float32)
        hidden = (stream_ref[rows].astype(jnp.float32) + mixed.T).astype(jnp.bfloat16)
        hid_ref[rows] = hidden
        pvel[hx] += jnp.dot(wlat_ref[:, rows], hidden, preferred_element_type=jnp.float32)

    def pv_copy(step):
        return pltpu.make_async_remote_copy(
            src_ref=pvel.at[hx], dst_ref=pvel.at[hx],
            send_sem=pv_send.at[step - 1], recv_sem=pv_recv.at[step - 1],
            device_id={"heads": lax.rem(hx + step, nh)}, device_id_type=MESH)

    for step in range(1, nh):
        pv_copy(step).start()

    @pl.when(jnp.logical_not(links[1]))
    def _():
        dext[:, pl.ds(0, 2 * FT)] = jnp.zeros((dext.shape[0], 2 * FT), dext.dtype)

    @pl.loop(0, heads_here)
    def _(c):
        for side in range(2):
            @pl.when(links[side])
            def _():
                msg_copy(side, c).wait_send()
        for step in range(1, nh):
            at_copy(step, c).wait_send()

    for c in range(LAG):
        for side in range(2):
            @pl.when(links[side])
            def _():
                tail_copy(side, c).wait_send()

    for step in range(1, nh):
        for piece in range(PIECES):
            w_copy(step, piece).wait_send()
            for hop in range(1, ng):
                g_copy(step, hop, piece).wait_send()
            for group in range(ng):
                sib_copy(step, group, piece).wait_send()

    for step in range(1, nh):
        pv_copy(step).wait_recv()
    velocity = pvel[0]
    for p in range(1, nh):
        velocity = velocity + pvel[p]
    dext[:, pl.ds(2 * FT, tok)] = (lat_ref[...] + step_size * velocity).astype(jnp.bfloat16)
    last = pltpu.make_async_remote_copy(
        src_ref=dext.at[:, pl.ds(tok, 2 * FT)], dst_ref=dext.at[:, pl.ds(0, 2 * FT)],
        send_sem=d_send, recv_sem=d_recv, device_id={"frames": me + 1}, device_id_type=MESH)

    @pl.when(links[0])
    def _():
        last.start()

    for step in range(1, nh):
        pv_copy(step).wait_send()

    @pl.when(links[1])
    def _():
        last.wait_recv()

    den_ref[...] = dext[...]

    @pl.when(links[0])
    def _():
        last.wait_send()


def conv_kernel(fh, clip_ref, den_ref, w_ref, bias_ref, hid_ref, out_ref, hid_out, patch, held, sem):
    load_hidden = pltpu.make_async_copy(hid_ref, held, sem.at[0])
    load_hidden.start()
    save_hidden = pltpu.make_async_copy(held, hid_out, sem.at[1])
    first = lax.axis_index("frames") * fh
    pix = 4 * FT
    row64 = lax.broadcasted_iota(jnp.int32, (LAT_CH, 4 * LAT_CH), 1)
    ch = lax.broadcasted_iota(jnp.int32, (LAT_CH, 4 * LAT_CH), 0)
    tokn = lax.broadcasted_iota(jnp.int32, (FT, pix), 0)
    where = lax.broadcasted_iota(jnp.int32, (FT, pix), 1)
    lane = lax.broadcasted_iota(jnp.int32, (LAT_CH, pix), 1)
    width = 2 * FW
    ypos, xpos = lane // width, lane % width
    selects, places = [], []
    for phase in range(4):
        p, q = phase // 2, phase % 2
        selects.append((row64 == 4 * ch + phase).astype(jnp.bfloat16))
        target = (2 * (tokn // FW) + p) * width + 2 * (tokn % FW) + q
        places.append((where == target).astype(jnp.bfloat16))
    for e in range(fh + 2):
        frame = den_ref[:, pl.ds(e * FT, FT)]
        image = jnp.zeros((LAT_CH, pix), jnp.float32)
        for phase in range(4):
            rows = jnp.dot(selects[phase], frame, preferred_element_type=jnp.float32).astype(jnp.bfloat16)
            image = image + jnp.dot(rows, places[phase], preferred_element_type=jnp.float32)
        for i in range(3):
            for j in range(3):
                shift = (i - 1) * width + (j - 1)
                moved = pltpu.roll(image, (-shift) % pix, 1) if shift else image
                ok = ((ypos + (i - 1) >= 0) & (ypos + (i - 1) < 2 * FH)
                      & (xpos + (j - 1) >= 0) & (xpos + (j - 1) < width))
                patch[e, pl.ds((3 * i + j) * LAT_CH, LAT_CH)] = jnp.where(ok, moved, 0.0).astype(jnp.bfloat16)
    load_hidden.wait()
    save_hidden.start()
    bias = bias_ref[...].T
    for f in range(fh):
        here = clip_ref[0, first + f]
        back1 = jnp.where((first + f >= 1) & (clip_ref[0, jnp.maximum(first + f - 1, 0)] == here), 1, 0)
        back2 = jnp.where((first + f >= 2) & (clip_ref[0, jnp.maximum(first + f - 2, 0)] == here), 2, back1)
        rows = jnp.concatenate([patch[f + 2 - back2], patch[f + 2 - back1], patch[f + 2]], axis=0)
        conv = lax.dot_general(w_ref[...], rows, (((0,), (0,)), ((), ())), preferred_element_type=jnp.float32)
        out_ref[f] = (conv + bias).astype(jnp.bfloat16)
    save_hidden.wait()


def shards(n, nh, ng, np_, query, key, value, stream, w_out, w_lat, latent, frame_clip, w_conv, conv_bias):
    tok, feats = query.shape[1:]
    fh = tok // FT
    seq_frames = frame_clip.shape[1]
    halo = seq_frames // 2 - 1
    hops = -(-halo // fh)
    chunks = feats // HD // CHUNK
    model, mcols = w_out.shape[1], stream.shape[1]
    latp = w_lat.shape[1]
    ext = (2 * halo + fh) * FT
    vmem = pl.BlockSpec(memory_space=pltpu.VMEM)
    hbm = pl.BlockSpec(memory_space=pl.ANY)
    smem = pl.BlockSpec(memory_space=pltpu.SMEM)
    peers = max(1, nh - 1)
    dma = pltpu.SemaphoreType.DMA
    heads_here = feats // HD
    results = (jax.ShapeDtypeStruct((mcols, tok), jnp.bfloat16),
               jax.ShapeDtypeStruct((latp, tok + 2 * FT), jnp.bfloat16))
    params = pltpu.CompilerParams(collective_id=0, has_side_effects=True, vmem_limit_bytes=56 * 1024 * 1024)
    operands = (frame_clip, query[0], key[0], value[0], stream[0], w_out, w_lat.T, latent[0])
    pack = pl.pallas_call(
        functools.partial(pack_kernel, n, nh, ng, np_, fh),
        out_shape=results,
        in_specs=[smem, vmem, vmem, vmem, vmem, hbm, vmem, vmem],
        out_specs=(vmem, vmem),
        scratch_shapes=[
            pltpu.VMEM((fh + 4, 3 * fh * FT), jnp.float32),
            pltpu.VMEM((2, heads_here, 2 * fh * FT, HD), jnp.bfloat16),
            pltpu.VMEM((2, heads_here, 2 * fh * FT, HD), jnp.bfloat16),
            pltpu.VMEM((2, LAG, 2 * FT, HD), jnp.bfloat16),
            pltpu.VMEM((2, LAG, 2 * FT, HD), jnp.bfloat16),
            pltpu.VMEM((2, heads_here, 2 * FT, HD), jnp.bfloat16),
            pltpu.VMEM((tok, nh * feats), jnp.bfloat16),
            pltpu.VMEM((nh * feats, mcols), jnp.bfloat16),
            pltpu.VMEM((nh, latp, tok), jnp.float32),
            pltpu.VMEM((latp, tok + 2 * FT), jnp.bfloat16),
            dma((2, heads_here)), dma((2, heads_here)),
            dma((2, LAG)), dma((2, LAG)),
            dma((peers, heads_here)), dma((peers, heads_here)),
            dma((peers, PIECES)), dma((peers, PIECES)),
            dma((peers, ng, PIECES)), dma((peers, ng, PIECES)),
            dma((peers, ng, PIECES)), dma((peers, ng, PIECES)),
            dma((peers,)), dma((peers,)),
            dma(()), dma(()), dma(()),
        ],
        compiler_params=params,
        name="clip_pack",
    )
    chain = pl.pallas_call(
        functools.partial(block_kernel, n, nh, np_, halo, fh),
        out_shape=results,
        in_specs=[smem, vmem, hbm, hbm, vmem, hbm, vmem, vmem],
        out_specs=(vmem, vmem),
        scratch_shapes=[
            pltpu.VMEM((fh, (2 * halo + 1) * FT), jnp.float32),
            pltpu.VMEM((ext, feats), jnp.bfloat16),
            pltpu.VMEM((ext, feats), jnp.bfloat16),
            pltpu.VMEM((tok, nh * feats), jnp.bfloat16),
            pltpu.VMEM((nh * feats, mcols), jnp.bfloat16),
            pltpu.VMEM((nh, latp, tok), jnp.float32),
            pltpu.VMEM((latp, tok + 2 * FT), jnp.bfloat16),
            dma((2, hops, chunks, 2)), dma((2, hops, chunks, 2)),
            dma((peers, chunks)), dma((peers, chunks)),
            dma((peers,)), dma((peers,)),
            dma((peers,)), dma((peers,)),
            dma((peers,)), dma((peers,)),
            dma(()), dma(()), dma((3,)),
        ],
        compiler_params=params,
        name="clip_block",
    )
    fits = fh == 3 and seq_frames // 2 <= 2 * fh
    hidden, den = (pack if fits else chain)(*operands)

    outs = w_conv.shape[0]
    feat, hidden = pl.pallas_call(
        functools.partial(conv_kernel, fh),
        out_shape=(jax.ShapeDtypeStruct((fh, outs, 4 * FT), jnp.bfloat16),
                   jax.ShapeDtypeStruct((mcols, tok), jnp.bfloat16)),
        in_specs=[smem, vmem, vmem, vmem, hbm],
        out_specs=(vmem, hbm),
        scratch_shapes=[pltpu.VMEM((fh + 2, 9 * LAT_CH, 4 * FT), jnp.bfloat16),
                        pltpu.VMEM((mcols, tok), jnp.bfloat16), dma((2,))],
        name="causal_conv",
    )(frame_clip, den, w_conv.T, conv_bias[None, :], hidden)
    return (hidden[None], jnp.transpose(feat, (1, 0, 2))[None])


def solution(mesh):
    sizes = dict(mesh.shape)
    return jax.shard_map(
        functools.partial(shards, sizes["frames"], sizes["heads"], sizes["groups"], sizes["pipe"]),
        mesh=mesh,
        in_specs=(
            P(("groups", "pipe"), "frames", "heads"),
            P(("groups", "pipe"), "frames", "heads"),
            P(("groups", "pipe"), "frames", "heads"),
            P(("groups", "pipe"), "heads", "frames"),
            P("heads", None),
            P("heads", None),
            P(("groups", "pipe"), None, "frames"),
            P(("groups", "pipe"), None),
            P("heads", None),
            P("heads"),
        ),
        out_specs=(
            P(("groups", "pipe"), "heads", "frames"),
            P(("groups", "pipe"), "heads", "frames", None),
        ),
        check_vma=False,
    )
```
